256 devices in a mesh: ctx: 32 (over x_lo, z, core), ep: 8 (over y, x_hi).
Axes of the slice: x: 4 (x_hi: 2, x_lo: 2; x = x_hi * 2 + x_lo), y: 4, z: 8, core: 2. Of those that a mesh axis runs over, the one named last changes fastest.
Arguments:
- queries: bfloat16 [4096, 6144], P('ctx', 'ep'), may hold values from -8 to 8
- keys: bfloat16 [4096, 1024], P('ctx', 'ep'), may hold values from -4 to 4
- values: bfloat16 [4096, 1024], P('ctx', 'ep'), may hold values from -13.5 to 13.5
- gate_weight: bfloat16 [32, 6144, 2048], P('ctx', 'ep'), may hold values from -0.078125 to 0.078125
- up_weight: bfloat16 [32, 6144, 2048], P('ctx', 'ep'), may hold values from -0.078125 to 0.078125
- down_weight: bfloat16 [32, 2048, 6144], P('ctx', None, 'ep'), may hold values from -0.125 to 0.125
- expert_ids: int32 [4096, 2], P('ctx'), may hold values from 0 to 31, as said below
- route_logits: float32 [4096, 2], P('ctx'), may hold values from -6 to 6
Outputs:
- layer_out: bfloat16 [4096, 6144], P('ctx', 'ep')
The draws below stay inside these ranges and needn't reach their ends.
Inputs may be any that keep to these rules, and one draw needn't show every extreme that they name: `expert_ids`: the two experts of a position differ. In every sequence block of 128 positions the same 2 experts are named exactly 24 times each, one further expert is named exactly 12 times, and every other expert is named at least once and at most 12 times.
All inputs are finite; a program needn't handle non-finite values.
Results may differ from the reference program's by a relative error of at most 0.017.
Values may be sent and summed in bfloat16 or wider, within the bound.
No kernel may reach another device: no remote copies, remote signals or barrier semaphores. Data moves between devices by JAX's collectives and lax.ppermute only.
A program may use at most 64 MiB of HBM per device.

```python
import jax
import jax.numpy as jnp
from jax import lax

D = 6144
H = 48
KVH = 8
HD = 128
FF = 2048
HOT = 2
TOK_DEV = 128
TOKENS = 4096
EXPERTS = 32
CAP_HOT = 24
CAP_COLD = 12
N_CTX = 32


def draw_queries(key, part):
    sample = jnp.clip(1.4 * jax.random.normal(jax.random.fold_in(key, 1), (TOKENS, H * HD), jnp.float32), -4.0, 4.0)
    return sample.astype(jnp.bfloat16)


def draw_keys(key, part):
    sample = jnp.clip(1.4 * jax.random.normal(jax.random.fold_in(key, 2), (TOKENS, KVH * HD), jnp.float32), -4.0, 4.0)
    return sample.astype(jnp.bfloat16)


def draw_values(key, part):
    channel_sign = jnp.where(jax.random.bernoulli(jax.random.fold_in(key, 31), 0.5, (KVH * HD,)), 1.0, -1.0).astype(jnp.float32)
    level = jnp.full((KVH * HD,), 1.5, jnp.float32)
    noise = jnp.clip(3.0 * jax.random.normal(jax.random.fold_in(key, 33), (TOKENS, KVH * HD), jnp.float32), -12.0, 12.0)
    sample = (channel_sign * level)[None, :] + noise
    return sample.astype(jnp.bfloat16)


def draw_expert_ids(key, part):
    ordering = jax.random.permutation(jax.random.fold_in(key, 21), EXPERTS).astype(jnp.int32)
    others = EXPERTS - HOT - 1
    remain = 2 * TOK_DEV - HOT * CAP_HOT - CAP_COLD

    def one_block(block):
        block_key = jax.random.fold_in(jax.random.fold_in(key, 22), block)
        shuffle = jax.random.permutation(jax.random.fold_in(block_key, 1), others).astype(jnp.int32)
        picks = jnp.arange(2 * TOK_DEV, dtype=jnp.int32)
        beyond = picks - HOT * CAP_HOT - CAP_COLD
        spread = jnp.clip(beyond, 0, remain - 1) * others // remain
        chosen_rank = jnp.where(picks < HOT * CAP_HOT, picks // CAP_HOT, jnp.where(beyond < 0, HOT, HOT + 1 + shuffle[spread]))
        listed = ordering[chosen_rank]
        paired = jnp.stack([listed[:TOK_DEV], listed[TOK_DEV:]], axis=1)
        mover = jax.random.permutation(jax.random.fold_in(block_key, 2), TOK_DEV)
        paired = paired[mover]
        flipper = jax.random.randint(jax.random.fold_in(block_key, 3), (TOK_DEV, 1), 0, 2)
        return jnp.where(flipper == 1, paired[:, ::-1], paired)
    blocks = jax.vmap(one_block)(jnp.arange(N_CTX, dtype=jnp.int32))
    return blocks.reshape(TOKENS, 2).astype(jnp.int32)


def steps_of(stream_key, dims, shards, least, largest):
    loudness, own = 1.0, jax.random.fold_in(stream_key, 6)
    for axis_at, parts in shards:
        steps = jnp.exp(jax.random.uniform(jax.random.fold_in(own, axis_at), (parts,), jnp.float32, least / len(shards), largest / len(shards)))
        loudness = loudness * jnp.repeat(steps, dims[axis_at] // parts).reshape([-1 if axis == axis_at else 1 for axis in range(len(dims))])
    return loudness


def gaussian(own_key, shape, deviation, most, pieces=(), held_as=jnp.bfloat16):
    loudness = steps_of(own_key, shape, pieces, -0.22, 0.18) if pieces else 1.0
    array = jax.random.normal(own_key, shape, jnp.float32) * deviation * loudness
    return jnp.minimum(jnp.maximum(array, -most), most).astype(held_as)


def setup_inputs(seed: int = 0) -> dict:
    seeds = jax.random.split(jax.random.key(seed), 9)
    return {
        "queries": draw_queries(jax.random.fold_in(seeds[8], 71), 0),
        "keys": draw_keys(jax.random.fold_in(seeds[8], 71), 0),
        "values": draw_values(jax.random.fold_in(seeds[8], 71), 0),
        "gate_weight": gaussian(seeds[3], (EXPERTS, D, FF), D ** -0.5, 0.078125, ((0, 32), (1, 8))),
        "up_weight": gaussian(seeds[4], (EXPERTS, D, FF), D ** -0.5, 0.078125, ((0, 32), (1, 8))),
        "down_weight": gaussian(seeds[5], (EXPERTS, FF, D), FF ** -0.5, 0.125, ((0, 32), (2, 8))),
        "expert_ids": draw_expert_ids(jax.random.fold_in(seeds[8], 71), 0),
        "route_logits": gaussian(seeds[7], (TOKENS, 2), 1.0, 6.0, ((0, 32),), jnp.float32),
    }


def attention_heads(queries, keys, values):
    length = queries.shape[0]
    groups = H // KVH
    score_scale = HD ** -0.5
    query_heads = queries.reshape(length, H, HD).transpose(1, 0, 2)
    key_heads = jnp.repeat(keys.reshape(length, KVH, HD).transpose(1, 0, 2), groups, axis=0)
    value_heads = jnp.repeat(values.reshape(length, KVH, HD).transpose(1, 0, 2), groups, axis=0)
    position = jnp.arange(length, dtype=jnp.int32)
    allowed = position[:, None] >= position[None, :]

    def one_head(operands):
        query_h, key_h, value_h = operands
        scores = jnp.dot(query_h, key_h.T, preferred_element_type=jnp.float32) * score_scale
        scores = jnp.where(allowed, scores, -jnp.inf)
        row_top = jnp.max(scores, axis=1, keepdims=True)
        weights = jnp.exp(scores - row_top)
        row_total = jnp.sum(weights, axis=1, keepdims=True)
        mixture = jnp.dot(weights.astype(jnp.bfloat16), value_h, preferred_element_type=jnp.float32)
        return mixture / row_total

    head_out = lax.map(one_head, (query_heads, key_heads, value_heads))
    return head_out.transpose(1, 0, 2).reshape(length, H * HD).astype(jnp.bfloat16)


def reference(queries, keys, values, gate_weight, up_weight, down_weight, expert_ids, route_logits):
    attended = attention_heads(queries, keys, values)
    route_share = jax.nn.softmax(route_logits.astype(jnp.float32), axis=-1).reshape(-1)
    flat_ids = expert_ids.reshape(-1)
    slot_count = N_CTX * CAP_HOT

    def one_expert(mixture, operands):
        expert, gate_w, up_w, down_w = operands
        hit_mask = flat_ids == expert
        where_hit = jnp.nonzero(hit_mask, size=slot_count, fill_value=0)[0].astype(jnp.int32)
        live_slot = jnp.arange(slot_count, dtype=jnp.int32) < jnp.sum(hit_mask.astype(jnp.int32))
        token_index = where_hit // 2
        chosen = attended[token_index]
        gate_sum = jnp.dot(chosen, gate_w, preferred_element_type=jnp.float32)
        up_sum = jnp.dot(chosen, up_w, preferred_element_type=jnp.float32)
        hidden = (jax.nn.silu(gate_sum) * up_sum).astype(jnp.bfloat16)
        answer = jnp.dot(hidden, down_w, preferred_element_type=jnp.float32).astype(jnp.bfloat16)
        factor = jnp.where(live_slot, route_share[where_hit], jnp.zeros((), route_share.dtype))
        mixture = mixture.at[token_index].add(answer.astype(jnp.float32) * factor[:, None])
        return mixture, None

    start_mixture = jnp.zeros((TOKENS, D), jnp.float32)
    mixture, unused = lax.scan(one_expert, start_mixture, (jnp.arange(EXPERTS, dtype=jnp.int32), gate_weight, up_weight, down_weight))
    return (attended.astype(jnp.float32) + mixture).astype(jnp.bfloat16)
```

```python
import functools

import jax
import jax.numpy as jnp
from jax import lax
from jax.experimental import pallas as pl
from jax.experimental.pallas import tpu as pltpu
from jax.sharding import PartitionSpec as P


BF = jnp.bfloat16
F32 = jnp.float32
H = 48
KVH = 8
HD = 128
TOK = 128
NCTX = 32
NEP = 8
SLOTS = 24
Z = 8
NEG = -1e30


def place(xl, z, c):
    return xl * 2 * Z + z * 2 + c


def z_shift(k):
    return [
        (place(xl, z, c), place(xl, (z + k) % Z, c))
        for xl in range(2)
        for z in range(Z)
        for c in range(2)
    ]


CORE_PAIRS = [(i, i ^ 1) for i in range(NCTX)]
XLO_PAIRS = [(i, i ^ (2 * Z)) for i in range(NCTX)]
Z_STEPS = (7, 1, 6, 2, 5, 3, 4)


def gather_kv(kv):
    near = [kv] + [lax.ppermute(kv, "ctx", z_shift(k)) for k in Z_STEPS]
    far = [lax.ppermute(block, "ctx", XLO_PAIRS) for block in near]
    mine = jnp.concatenate(near + far, axis=0)
    other = lax.ppermute(mine, "ctx", CORE_PAIRS)
    return mine, other


def block_sources(my):
    xl, z, c = my // (2 * Z), (my // 2) % Z, my % 2
    order = []
    for cc in (c, 1 - c):
        for xx in (xl, 1 - xl):
            for k in (0,) + Z_STEPS:
                order.append(place(xx, (z + Z - k) % Z, cc))
    return jnp.stack(order + [my]).astype(jnp.int32)


def ranks(first_line, second_line, first_col, second_col, axis):
    a = lax.broadcasted_iota(jnp.int32, (TOK, TOK), axis)
    b = lax.broadcasted_iota(jnp.int32, (TOK, TOK), 1 - axis)
    before = a < b
    if axis == 0:
        own0, own1, oth0, oth1 = first_line, second_line, first_col, second_col
    else:
        own0, own1, oth0, oth1 = first_col, second_col, first_line, second_line

    def count(mask):
        return jnp.sum(mask.astype(F32), axis=axis, keepdims=True).astype(jnp.int32)

    rank0 = count((oth0 == own0) & before)
    rank1 = count(oth0 == own1) + count((oth1 == own1) & before)
    return own0, own1, rank0, rank1


def attend_kernel(meta, q, ka, kb, id_line, id_col, att, placed, s, m, total, acc, q6):
    my = meta[NCTX]
    for h in range(6):
        q6[pl.ds(h * TOK, TOK), :] = q[:, h * HD : (h + 1) * HD]
    m[...] = jnp.full_like(m, NEG)
    gap = (lax.broadcasted_iota(jnp.int32, (6 * TOK, TOK), 0) & (TOK - 1)) - lax.broadcasted_iota(
        jnp.int32, (6 * TOK, TOK), 1
    )
    scale = HD ** (-0.5)
    half = NCTX // 2 * TOK
    for side, kv in ((0, ka), (1, kb)):

        def scores(i, carry):
            rows = pl.ds(pl.multiple_of(i * 2 * TOK, 2 * TOK), 2 * TOK)
            cols = pl.ds(pl.multiple_of(side * half + i * 2 * TOK, 2 * TOK), 2 * TOK)
            value = lax.dot_general(
                q6[...], kv[rows, 0:HD], (((1,), (1,)), ((), ())), preferred_element_type=F32
            )
            base = side * (NCTX // 2) + i * 2
            left = jnp.where(gap >= (meta[base] - my) * TOK, value[:, :TOK], NEG)
            right = jnp.where(gap >= (meta[base + 1] - my) * TOK, value[:, TOK:], NEG)
            s[:, cols] = jnp.concatenate([left, right], axis=1)
            m[...] = jnp.maximum(m[...], jnp.maximum(left, right))
            return carry

        lax.fori_loop(0, NCTX // 4, scores, 0)
    top = jnp.broadcast_to(jnp.max(m[...], axis=1, keepdims=True), (6 * TOK, TOK))
    m[...] = top
    total[...] = jnp.zeros_like(total)
    acc[...] = jnp.zeros_like(acc)
    for side, kv in ((0, ka), (1, kb)):

        def mix(i, carry):
            rows = pl.ds(pl.multiple_of(i * 2 * TOK, 2 * TOK), 2 * TOK)
            cols = pl.ds(pl.multiple_of(side * half + i * 2 * TOK, 2 * TOK), 2 * TOK)
            part = s[:, cols]
            left = jnp.exp((part[:, :TOK] - m[...]) * scale)
            right = jnp.exp((part[:, TOK:] - m[...]) * scale)
            total[...] += left + right
            p = jnp.concatenate([left.astype(BF), right.astype(BF)], axis=1)
            acc[...] += jnp.dot(p, kv[rows, HD:], preferred_element_type=F32)
            return carry

        lax.fori_loop(0, NCTX // 4, mix, 0)
    out = (acc[...] / jnp.sum(total[...], axis=1, keepdims=True)).astype(BF)
    for h in range(6):
        att[:, h * HD : (h + 1) * HD] = out[h * TOK : (h + 1) * TOK]
    id0, id1, r0, r1 = ranks(
        id_line[0:1, :], id_line[1:2, :], id_col[:, 0:1], id_col[:, 1:2], 0
    )
    slot = lax.broadcasted_iota(jnp.int32, (NCTX * SLOTS, TOK), 0)
    pick = (slot == id0 * SLOTS + r0) | (slot == id1 * SLOTS + r1)
    pick = pick.astype(F32).astype(BF)
    placed[...] = jnp.dot(pick, att[...], preferred_element_type=F32).astype(BF)


VM = pl.BlockSpec(memory_space=pltpu.VMEM)
PARAMS = pltpu.CompilerParams(vmem_limit_bytes=56 * 1024 * 1024)


def attend(meta, q, ka, kb, id_line, id_col):
    return pl.pallas_call(
        attend_kernel,
        name="attend",
        out_shape=(
            jax.ShapeDtypeStruct((TOK, 6 * HD), BF),
            jax.ShapeDtypeStruct((NCTX * SLOTS, 6 * HD), BF),
        ),
        in_specs=[pl.BlockSpec(memory_space=pltpu.SMEM)] + [VM] * 5,
        out_specs=(VM, VM),
        scratch_shapes=[
            pltpu.VMEM((6 * TOK, NCTX * TOK), F32),
            pltpu.VMEM((6 * TOK, TOK), F32),
            pltpu.VMEM((6 * TOK, TOK), F32),
            pltpu.VMEM((6 * TOK, HD), F32),
            pltpu.VMEM((6 * TOK, HD), BF),
        ],
        compiler_params=PARAMS,
    )(meta, q, ka, kb, id_line, id_col)


def gate_up_kernel(x, wg, wu, out):
    width = wg.shape[2]
    out[0, :, :width] = jnp.dot(x[...], wg[0], preferred_element_type=F32).astype(BF)
    out[0, :, width:] = jnp.dot(x[...], wu[0], preferred_element_type=F32).astype(BF)


def gate_up(x, wg, wu):
    rows, depth = x.shape
    width = wg.shape[2] // NEP
    weight = pl.BlockSpec((1, depth, width), lambda j: (0, 0, j))
    return pl.pallas_call(
        gate_up_kernel,
        name="gate_up",
        grid=(NEP,),
        out_shape=jax.ShapeDtypeStruct((NEP, rows, 2 * width), BF),
        in_specs=[pl.BlockSpec((rows, depth), lambda j: (0, 0)), weight, weight],
        out_specs=pl.BlockSpec((1, rows, 2 * width), lambda j: (j, 0, 0)),
        compiler_params=PARAMS,
    )(x, wg, wu)


def hidden_kernel(parts, out):
    width = out.shape[2]
    total = parts[0].astype(F32)
    for j in range(1, NEP):
        total += parts[j].astype(F32)
    gate, up = total[:, :width], total[:, width:]
    value = (gate / (1.0 + jnp.exp(-gate)) * up).astype(BF)
    for j in range(NEP):
        out[j] = value


def hidden(parts):
    _, rows, width = parts.shape
    tile = 64
    return pl.pallas_call(
        hidden_kernel,
        name="hidden",
        grid=(rows // tile,),
        out_shape=jax.ShapeDtypeStruct((NEP, rows, width // 2), BF),
        in_specs=[pl.BlockSpec((NEP, tile, width), lambda i: (0, i, 0))],
        out_specs=pl.BlockSpec((NEP, tile, width // 2), lambda i: (0, i, 0)),
        compiler_params=PARAMS,
    )(parts)


def down_kernel(h, w, out, acc):
    j = pl.program_id(0)
    part = jnp.dot(h[0], w[0], preferred_element_type=F32)

    @pl.when(j == 0)
    def _():
        acc[...] = part

    @pl.when(j > 0)
    def _():
        acc[...] += part

    @pl.when(j == NEP - 1)
    def _():
        out[...] = acc[...].astype(BF)


def down(h, w):
    _, rows, width = h.shape
    cols = w.shape[2]
    return pl.pallas_call(
        down_kernel,
        name="down",
        grid=(NEP,),
        out_shape=jax.ShapeDtypeStruct((rows, cols), BF),
        in_specs=[
            pl.BlockSpec((1, rows, width), lambda j: (j, 0, 0)),
            pl.BlockSpec((1, width, cols), lambda j: (0, j, 0)),
        ],
        out_specs=pl.BlockSpec((rows, cols), lambda j: (0, 0)),
        scratch_shapes=[pltpu.VMEM((rows, cols), F32)],
        compiler_params=PARAMS,
    )(h, w)


def combine_kernel(answers, att, logits, id_line, id_col, out):
    id0, id1, r0, r1 = ranks(
        id_line[0:1, :], id_line[1:2, :], id_col[:, 0:1], id_col[:, 1:2], 1
    )
    slot = lax.broadcasted_iota(jnp.int32, (TOK, NCTX * SLOTS), 1)
    pick0 = (slot == id0 * SLOTS + r0).astype(F32).astype(BF)
    pick1 = (slot == id1 * SLOTS + r1).astype(F32).astype(BF)
    l0, l1 = logits[:, 0:1], logits[:, 1:2]
    top = jnp.maximum(l0, l1)
    e0, e1 = jnp.exp(l0 - top), jnp.exp(l1 - top)
    both = e0 + e1
    first = jnp.dot(pick0, answers[...], preferred_element_type=F32) * (e0 / both)
    second = jnp.dot(pick1, answers[...], preferred_element_type=F32) * (e1 / both)
    out[...] = (att[...].astype(F32) + first + second).astype(BF)


def combine(answers, att, logits, id_line, id_col):
    return pl.pallas_call(
        combine_kernel,
        name="combine",
        out_shape=jax.ShapeDtypeStruct(att.shape, BF),
        in_specs=[VM] * 5,
        out_specs=VM,
        compiler_params=PARAMS,
    )(answers, att, logits, id_line, id_col)


def on_device(queries, keys, values, gate_weight, up_weight, down_weight, expert_ids, route_logits):
    my = lax.axis_index("ctx")
    id_line = expert_ids.T
    kv = jnp.concatenate([keys, values], axis=1)
    mine, other = gather_kv(kv)
    att, placed = attend(block_sources(my), queries, mine, other, id_line, expert_ids)
    outgoing = placed.reshape(NCTX, SLOTS, placed.shape[1])
    arrived = lax.all_to_all(outgoing, "ctx", 0, 0, tiled=True)
    parts = gate_up(arrived.reshape(NCTX * SLOTS, -1), gate_weight, up_weight)
    parts = lax.all_to_all(parts, "ep", 0, 0, tiled=True)
    pieces = lax.all_to_all(hidden(parts), "ep", 0, 0, tiled=True)
    produced = down(pieces, down_weight)
    back = lax.all_to_all(produced.reshape(NCTX, SLOTS, -1), "ctx", 0, 0, tiled=True)
    return combine(back.reshape(NCTX * SLOTS, -1), att, route_logits, id_line, expert_ids)


def solution(mesh):
    in_specs = (
        P("ctx", "ep"),
        P("ctx", "ep"),
        P("ctx", "ep"),
        P("ctx", "ep", None),
        P("ctx", "ep", None),
        P("ctx", None, "ep"),
        P("ctx", None),
        P("ctx", None),
    )
    return jax.shard_map(
        on_device, mesh=mesh, in_specs=in_specs, out_specs=P("ctx", "ep"), check_vma=False
    )
```

```python
import functools

import jax
import jax.numpy as jnp
from jax import lax
from jax.experimental import pallas as pl
from jax.experimental.pallas import tpu as pltpu
from jax.sharding import PartitionSpec as P


BF = jnp.bfloat16
F32 = jnp.float32
H = 48
KVH = 8
HD = 128
TOK = 128
NCTX = 32
NEP = 8
SLOTS = 24
Z = 8
NEG = -1e30
LOG2E = 1.4426950408889634
BLOCKS = 4
CAP = 12
THIRD = 256
SLOT = 18
SPAN = 56
ROWS = NCTX * SPAN
COLD = NCTX * CAP
EXTRA = NCTX * (SLOT - CAP)
TILE = 64
VM = pl.BlockSpec(memory_space=pltpu.VMEM)
ANY = pl.BlockSpec(memory_space=pl.ANY)


def room(mib):
    return pltpu.CompilerParams(vmem_limit_bytes=mib * 1024 * 1024)


def place(xl, z, c):
    return xl * 2 * Z + z * 2 + c


def z_shift(k):
    return [
        (place(xl, z, c), place(xl, (z + k) % Z, c))
        for xl in range(2)
        for z in range(Z)
        for c in range(2)
    ]


CORE_PAIRS = [(i, i ^ 1) for i in range(NCTX)]
XLO_PAIRS = [(i, i ^ (2 * Z)) for i in range(NCTX)]
Z_STEPS = (7, 1, 6, 2, 5, 3, 4)


def prepare_kernel(my, keys, values, id_line, kv, own, alone):
    kv[:, :HD] = keys[...]
    kv[:, HD:] = values[...]
    expert = lax.broadcasted_iota(jnp.int32, (NCTX, TOK), 0)
    named = (expert == id_line[0:1, :]).astype(F32) + (expert == id_line[1:2, :]).astype(F32)
    hot = (jnp.sum(named, axis=1, keepdims=True) > CAP).astype(jnp.int32)
    place_of = lax.broadcasted_iota(jnp.int32, (NCTX, 1), 0)
    own[0] = jnp.sum(hot * (place_of == my[0]).astype(jnp.int32))
    chip = hot * (place_of >> 1)
    low = jnp.max(chip + (1 - hot) * -1)
    high = jnp.min(chip + (1 - hot) * NCTX)
    alone[0] = (low == high).astype(jnp.int32)


def prepare(my, keys, values, id_line):
    return pl.pallas_call(
        prepare_kernel,
        name="prepare",
        out_shape=(
            jax.ShapeDtypeStruct((TOK, 2 * HD), BF),
            jax.ShapeDtypeStruct((1,), jnp.int32),
            jax.ShapeDtypeStruct((1,), jnp.int32),
        ),
        in_specs=[pl.BlockSpec(memory_space=pltpu.SMEM)] + [VM] * 3,
        out_specs=(VM,) + (pl.BlockSpec(memory_space=pltpu.SMEM),) * 2,
        compiler_params=room(4),
    )(my, keys, values, id_line)


def join_kernel(*refs):
    out = refs[-1]
    for b, ref in enumerate(refs[:-1]):
        out[b * TOK : (b + 1) * TOK] = ref[...]


def join(blocks):
    return pl.pallas_call(
        join_kernel,
        name="join",
        out_shape=jax.ShapeDtypeStruct((len(blocks) * TOK, 2 * HD), BF),
        in_specs=[VM] * len(blocks),
        out_specs=VM,
        compiler_params=room(6),
    )(*blocks)


def gather_kv(kv):
    near = [kv] + [lax.ppermute(kv, "ctx", z_shift(k)) for k in Z_STEPS]
    far = [lax.ppermute(block, "ctx", XLO_PAIRS) for block in near]
    mine = [join(near), join(far)]
    return mine + [lax.ppermute(part, "ctx", CORE_PAIRS) for part in mine]


def column(line):
    return jnp.transpose(jnp.broadcast_to(line.astype(F32), (TOK, TOK)))[:, 0:1]


def ranks(id_line, axis):
    a = lax.broadcasted_iota(jnp.int32, (TOK, TOK), axis)
    b = lax.broadcasted_iota(jnp.int32, (TOK, TOK), 1 - axis)
    before = a < b
    line0, line1 = id_line[0:1, :].astype(F32), id_line[1:2, :].astype(F32)
    col0, col1 = column(line0), column(line1)
    if axis == 0:
        own0, own1, oth0, oth1 = line0, line1, col0, col1
    else:
        own0, own1, oth0, oth1 = col0, col1, line0, line1

    def count(mask):
        return jnp.sum(mask.astype(F32), axis=axis, keepdims=True).astype(jnp.int32)

    rank0 = count((oth0 == own0) & before)
    rank1 = count(oth0 == own1) + count((oth1 == own1) & before)
    return own0.astype(jnp.int32), own1.astype(jnp.int32), rank0, rank1


def split_row(expert, rank):
    over = (rank >= SLOT).astype(jnp.int32)
    return (expert ^ over) * SPAN + rank - (SLOT - CAP) * over


def slot_map(c, extra, transposed):
    count = SLOT - CAP if extra else CAP
    rows, cols = 8 * count, 8 * SPAN
    shape = (cols, rows) if transposed else (rows, cols)
    i = lax.broadcasted_iota(jnp.int32, shape, 1 if transposed else 0)
    j = lax.broadcasted_iota(jnp.int32, shape, 0 if transposed else 1)
    source = (i * (43 if count == CAP else 86)) >> 9
    slot = i - source * count + (CAP if extra else 0)
    return (j == source * SPAN + c * SLOT + slot).astype(F32).astype(BF)


def place_kernel(att, id_line, placed):
    id0, id1, r0, r1 = ranks(id_line, 0)
    slot = lax.broadcasted_iota(jnp.int32, (NCTX * SLOTS, TOK), 0)
    pick = (slot == id0 * SLOTS + r0) | (slot == id1 * SLOTS + r1)
    pick = pick.astype(F32).astype(BF)
    placed[...] = jnp.dot(pick, att[...], preferred_element_type=F32).astype(BF)


def attend_kernel(
    my_ref, q, ka, kb, kc, kd, id_line, att, placed, s, m, total, acc, q6, meta
):
    my = my_ref[0]
    xl, z, core = my // (2 * Z), (my // 2) % Z, my % 2
    at = 0
    for cc in (core, 1 - core):
        for xx in (xl, 1 - xl):
            for k in (0,) + Z_STEPS:
                meta[at] = (place(xx, (z + Z - k) % Z, cc) - my) * TOK
                at += 1
    for h in range(6):
        q6[pl.ds(h * TOK, TOK), :] = q[:, h * HD : (h + 1) * HD]
    m[...] = jnp.full_like(m, NEG)
    gap = (lax.broadcasted_iota(jnp.int32, (6 * TOK, TOK), 0) & (TOK - 1)) - lax.broadcasted_iota(
        jnp.int32, (6 * TOK, TOK), 1
    )
    scale = HD ** (-0.5) * LOG2E
    quarter = NCTX // 4 * TOK
    wide = BLOCKS * TOK
    for side, kv in enumerate((ka, kb, kc, kd)):

        def scores(i, carry):
            rows = pl.ds(pl.multiple_of(i * wide, wide), wide)
            cols = pl.ds(pl.multiple_of(side * quarter + i * wide, wide), wide)
            value = lax.dot_general(
                q6[...], kv[rows, 0:HD], (((1,), (1,)), ((), ())), preferred_element_type=F32
            )
            base = side * (NCTX // 4) + i * BLOCKS
            pieces = [
                jnp.where(gap >= meta[base + b], value[:, b * TOK : (b + 1) * TOK], NEG)
                for b in range(BLOCKS)
            ]
            s[:, cols] = jnp.concatenate(pieces, axis=1)
            m[...] = jnp.maximum(m[...], functools.reduce(jnp.maximum, pieces))
            return carry

        lax.fori_loop(0, NCTX // 4 // BLOCKS, scores, 0)
    top = jnp.broadcast_to(jnp.max(m[...], axis=1, keepdims=True), (6 * TOK, TOK))
    m[...] = top
    total[...] = jnp.zeros_like(total)
    acc[...] = jnp.zeros_like(acc)
    for side, kv in enumerate((ka, kb, kc, kd)):

        def mix(i, carry):
            rows = pl.ds(pl.multiple_of(i * wide, wide), wide)
            cols = pl.ds(pl.multiple_of(side * quarter + i * wide, wide), wide)
            part = s[:, cols]
            top = m[...]
            pieces = [
                jnp.exp2((part[:, b * TOK : (b + 1) * TOK] - top) * scale) for b in range(BLOCKS)
            ]
            total[...] += functools.reduce(jnp.add, pieces)
            p = jnp.concatenate([piece.astype(BF) for piece in pieces], axis=1)
            acc[...] += jnp.dot(p, kv[rows, HD:], preferred_element_type=F32)
            return carry

        lax.fori_loop(0, NCTX // 4 // BLOCKS, mix, 0)
    out = (acc[...] / jnp.sum(total[...], axis=1, keepdims=True)).astype(BF)
    for h in range(6):
        att[:, h * HD : (h + 1) * HD] = out[h * TOK : (h + 1) * TOK]
    id0, id1, r0, r1 = ranks(id_line, 0)
    slot = lax.broadcasted_iota(jnp.int32, (ROWS, TOK), 0)
    row0, row1 = split_row(id0, r0), split_row(id1, r1)
    filled = jnp.zeros((ROWS, THIRD), F32)
    for c in range(3):
        pick = (slot == row0 + c * SLOT) | (slot == row1 + c * SLOT)
        pick = pick.astype(F32).astype(BF)
        filled += jnp.dot(pick, att[:, c * THIRD : (c + 1) * THIRD], preferred_element_type=F32)
    placed[...] = filled.astype(BF)


def attend(my, q, ka, kb, kc, kd, id_line):
    return pl.pallas_call(
        attend_kernel,
        name="attend",
        out_shape=(
            jax.ShapeDtypeStruct((TOK, 6 * HD), BF),
            jax.ShapeDtypeStruct((ROWS, THIRD), BF),
        ),
        in_specs=[pl.BlockSpec(memory_space=pltpu.SMEM)] + [VM] * 6,
        out_specs=(VM, VM),
        scratch_shapes=[
            pltpu.VMEM((6 * TOK, NCTX * TOK), F32),
            pltpu.VMEM((6 * TOK, TOK), F32),
            pltpu.VMEM((6 * TOK, TOK), F32),
            pltpu.VMEM((6 * TOK, HD), F32),
            pltpu.VMEM((6 * TOK, HD), BF),
            pltpu.SMEM((NCTX,), jnp.int32),
        ],
        compiler_params=room(28),
    )(my, q, ka, kb, kc, kd, id_line)


def gate_up_kernel(x, wg, wu, out):
    width = wg.shape[2]
    out[0, :, :width] = jnp.dot(x[...], wg[0], preferred_element_type=F32).astype(BF)
    out[0, :, width:] = jnp.dot(x[...], wu[0], preferred_element_type=F32).astype(BF)


def gate_up(x, wg, wu):
    rows, depth = x.shape
    width = wg.shape[2] // NEP
    weight = pl.BlockSpec((1, depth, width), lambda j: (0, 0, j))
    return pl.pallas_call(
        gate_up_kernel,
        name="gate_up",
        grid=(NEP,),
        out_shape=jax.ShapeDtypeStruct((NEP, rows, 2 * width), BF),
        in_specs=[pl.BlockSpec((rows, depth), lambda j: (0, 0)), weight, weight],
        out_specs=pl.BlockSpec((1, rows, 2 * width), lambda j: (j, 0, 0)),
        compiler_params=room(24),
    )(x, wg, wu)


def hidden_kernel(parts, out):
    width = out.shape[2]
    total = parts[0].astype(F32)
    for j in range(1, NEP):
        total += parts[j].astype(F32)
    gate, up = total[:, :width], total[:, width:]
    value = (gate / (1.0 + jnp.exp(-gate)) * up).astype(BF)
    for j in range(NEP):
        out[j] = value


def hidden(parts):
    _, rows, width = parts.shape
    tile = TILE if rows % 192 else 192
    return pl.pallas_call(
        hidden_kernel,
        name="hidden",
        grid=(rows // tile,),
        out_shape=jax.ShapeDtypeStruct((NEP, rows, width // 2), BF),
        in_specs=[pl.BlockSpec((NEP, tile, width), lambda i: (0, i, 0))],
        out_specs=pl.BlockSpec((NEP, tile, width // 2), lambda i: (0, i, 0)),
        compiler_params=room(12),
    )(parts)


def down_kernel(h, w, out, acc):
    j = pl.program_id(0)
    part = jnp.dot(h[0], w[0], preferred_element_type=F32)

    @pl.when(j == 0)
    def _():
        acc[...] = part

    @pl.when(j > 0)
    def _():
        acc[...] += part

    @pl.when(j == NEP - 1)
    def _():
        out[...] = acc[...].astype(BF)


def down(h, w):
    _, rows, width = h.shape
    cols = w.shape[2]
    return pl.pallas_call(
        down_kernel,
        name="down",
        grid=(NEP,),
        out_shape=jax.ShapeDtypeStruct((rows, cols), BF),
        in_specs=[
            pl.BlockSpec((1, rows, width), lambda j: (j, 0, 0)),
            pl.BlockSpec((1, width, cols), lambda j: (0, j, 0)),
        ],
        out_specs=pl.BlockSpec((rows, cols), lambda j: (0, 0)),
        scratch_shapes=[pltpu.VMEM((rows, cols), F32)],
        compiler_params=room(16),
    )(h, w)


def split_gate_up_kernel(own, arr, wg, wu, sg, su, out, x):
    width = wg.shape[2] // NEP
    n, m = 8 * CAP, 8 * (SLOT - CAP)
    for c in range(3):
        cols = slice(c * THIRD, (c + 1) * THIRD)
        cold, extra = slot_map(c, False, False), slot_map(c, True, False)
        for g in range(NCTX // 8):
            group = arr[g * 8 * SPAN : (g + 1) * 8 * SPAN]
            x[g * n : (g + 1) * n, cols] = jnp.dot(
                cold, group, preferred_element_type=F32
            ).astype(BF)
            x[COLD + g * m : COLD + (g + 1) * m, cols] = jnp.dot(
                extra, group, preferred_element_type=F32
            ).astype(BF)

    def piece(lo, hi, first, second):
        def one(j, carry):
            cols = pl.ds(pl.multiple_of(j * width, width), width)
            for at, w in ((0, first), (width, second)):
                out[j, lo:hi, at : at + width] = jnp.dot(
                    x[lo:hi], w[0, :, cols], preferred_element_type=F32
                ).astype(BF)
            return carry

        lax.fori_loop(0, NEP, one, 0)

    @pl.when(own[0] == 1)
    def _():
        piece(0, COLD + EXTRA, wg, wu)

    @pl.when(own[0] == 0)
    def _():
        piece(0, COLD, wg, wu)
        piece(COLD, COLD + EXTRA, sg, su)


def split_gate_up(own, arr, wg, wu, sg, su):
    _, depth, full = wg.shape
    rows = COLD + EXTRA
    return pl.pallas_call(
        split_gate_up_kernel,
        name="split_gate_up",
        out_shape=jax.ShapeDtypeStruct((NEP, rows, 2 * full // NEP), BF),
        in_specs=[pl.BlockSpec(memory_space=pltpu.SMEM)] + [VM] * 5,
        out_specs=VM,
        scratch_shapes=[pltpu.VMEM((rows, depth), BF)],
        compiler_params=room(30),
    )(own, arr, wg, wu, sg, su)


def split_down_kernel(own, h, w, v, out, wide, y):
    width = h.shape[2]
    for j in range(NEP):
        wide[:, j * width : (j + 1) * width] = h[j]

    def product(lo, hi, weights):
        def one(c, carry):
            cols = pl.ds(pl.multiple_of(c * THIRD, THIRD), THIRD)
            y[lo:hi, cols] = jnp.dot(
                wide[lo:hi], weights[0, :, cols], preferred_element_type=F32
            ).astype(BF)
            return carry

        lax.fori_loop(0, 3, one, 0)

    @pl.when(own[0] == 1)
    def _():
        product(0, COLD + EXTRA, w)

    @pl.when(own[0] == 0)
    def _():
        product(0, COLD, w)
        product(COLD, COLD + EXTRA, v)

    n, m = 8 * CAP, 8 * (SLOT - CAP)
    maps = [(slot_map(c, False, True), slot_map(c, True, True)) for c in range(3)]
    for g in range(NCTX // 8):
        total = jnp.zeros((8 * SPAN, THIRD), F32)
        for c in range(3):
            cols = slice(c * THIRD, (c + 1) * THIRD)
            cold, extra = maps[c]
            total += jnp.dot(cold, y[g * n : (g + 1) * n, cols], preferred_element_type=F32)
            total += jnp.dot(
                extra, y[COLD + g * m : COLD + (g + 1) * m, cols], preferred_element_type=F32
            )
        out[g * 8 * SPAN : (g + 1) * 8 * SPAN] = total.astype(BF)


def split_down(own, h, w, v):
    _, rows, width = h.shape
    _, depth, cols = w.shape
    return pl.pallas_call(
        split_down_kernel,
        name="split_down",
        out_shape=jax.ShapeDtypeStruct((ROWS, THIRD), BF),
        in_specs=[pl.BlockSpec(memory_space=pltpu.SMEM)] + [VM] * 3,
        out_specs=VM,
        scratch_shapes=[pltpu.VMEM((rows, depth), BF), pltpu.VMEM((rows, cols), BF)],
        compiler_params=room(20),
    )(own, h, w, v)


def shares(logits):
    l0, l1 = column(logits[0:1, :]), column(logits[1:2, :])
    top = jnp.maximum(l0, l1)
    e0, e1 = jnp.exp(l0 - top), jnp.exp(l1 - top)
    both = e0 + e1
    return e0 / both, e1 / both


def split_combine_kernel(answers, att, logits, id_line, out):
    id0, id1, r0, r1 = ranks(id_line, 1)
    slot = lax.broadcasted_iota(jnp.int32, (TOK, ROWS), 1)
    row0, row1 = split_row(id0, r0), split_row(id1, r1)
    s0, s1 = shares(logits)
    for c in range(3):
        cols = slice(c * THIRD, (c + 1) * THIRD)
        pick0 = (slot == row0 + c * SLOT).astype(F32).astype(BF)
        pick1 = (slot == row1 + c * SLOT).astype(F32).astype(BF)
        first = jnp.dot(pick0, answers[...], preferred_element_type=F32)
        second = jnp.dot(pick1, answers[...], preferred_element_type=F32)
        out[:, cols] = (att[:, cols].astype(F32) + first * s0 + second * s1).astype(BF)


def combine_kernel(answers, att, logits, id_line, out):
    id0, id1, r0, r1 = ranks(id_line, 1)
    slot = lax.broadcasted_iota(jnp.int32, (TOK, NCTX * SLOTS), 1)
    pick0 = (slot == id0 * SLOTS + r0).astype(F32).astype(BF)
    pick1 = (slot == id1 * SLOTS + r1).astype(F32).astype(BF)
    s0, s1 = shares(logits)
    first = jnp.dot(pick0, answers[...], preferred_element_type=F32) * s0
    second = jnp.dot(pick1, answers[...], preferred_element_type=F32) * s1
    out[...] = (att[...].astype(F32) + first + second).astype(BF)


def place_rows(att, id_line):
    return pl.pallas_call(
        place_kernel,
        name="place_rows",
        out_shape=jax.ShapeDtypeStruct((NCTX * SLOTS, att.shape[1]), BF),
        in_specs=[VM] * 2,
        out_specs=VM,
        compiler_params=room(8),
    )(att, id_line)


def combine(kernel, answers, att, logits, id_line):
    return pl.pallas_call(
        kernel,
        name="combine",
        out_shape=jax.ShapeDtypeStruct(att.shape, BF),
        in_specs=[VM] * 4,
        out_specs=VM,
        compiler_params=room(10),
    )(answers, att, logits, id_line)


def swap(x, axis):
    return lax.all_to_all(x, axis, 0, 0, tiled=True)


def owners_only(args):
    att, _, gate_weight, up_weight, down_weight, _, _, _, _, id_line, logits = args
    outgoing = place_rows(att, id_line).reshape(NCTX, SLOTS, att.shape[1])
    arrived = swap(outgoing, "ctx")
    parts = swap(gate_up(arrived.reshape(NCTX * SLOTS, -1), gate_weight, up_weight), "ep")
    produced = down(swap(hidden(parts), "ep"), down_weight)
    back = swap(produced.reshape(NCTX, SLOTS, -1), "ctx")
    return combine(combine_kernel, back.reshape(NCTX * SLOTS, -1), att, logits, id_line)


def both_cores(args):
    att, placed, wg, wu, wd, sg, su, sd, own, id_line, logits = args
    arrived = swap(placed.reshape(NCTX, SPAN, THIRD), "ctx").reshape(ROWS, THIRD)
    parts = swap(split_gate_up(own, arrived, wg, wu, sg, su), "ep")
    produced = split_down(own, swap(hidden(parts), "ep"), wd, sd)
    back = swap(produced.reshape(NCTX, SPAN, THIRD), "ctx").reshape(ROWS, THIRD)
    return combine(split_combine_kernel, back, att, logits, id_line)


def on_device(queries, keys, values, gate_weight, up_weight, down_weight, expert_ids, route_logits):
    my = lax.axis_index("ctx").astype(jnp.int32).reshape(1)
    id_line, logits = expert_ids.T, route_logits.T
    kv, own, one_chip = prepare(my, keys, values, id_line)
    parts = gather_kv(kv)
    theirs = [lax.ppermute(w, "ctx", CORE_PAIRS) for w in (gate_weight, up_weight, down_weight)]
    att, placed = attend(my, queries, *parts, id_line)
    args = (att, placed, gate_weight, up_weight, down_weight, *theirs, own, id_line, logits)
    return lax.cond(one_chip[0] == 1, owners_only, both_cores, args)


def solution(mesh):
    in_specs = (
        P("ctx", "ep"),
        P("ctx", "ep"),
        P("ctx", "ep"),
        P("ctx", "ep", None),
        P("ctx", "ep", None),
        P("ctx", None, "ep"),
        P("ctx", None),
        P("ctx", None),
    )
    return jax.shard_map(
        on_device, mesh=mesh, in_specs=in_specs, out_specs=P("ctx", "ep"), check_vma=False
    )
```

```python
import functools

import jax
import jax.numpy as jnp
from jax import lax
from jax.experimental import pallas as pl
from jax.experimental.pallas import tpu as pltpu
from jax.sharding import PartitionSpec as P


BF = jnp.bfloat16
F32 = jnp.float32
H = 48
KVH = 8
HD = 128
TOK = 128
NCTX = 32
NEP = 8
SLOTS = 24
Z = 8
NEG = -1e30
LOG2E = 1.4426950408889634
BLOCKS = 4
CAP = 12
THIRD = 256
SLOT = 18
SPAN = 56
ROWS = NCTX * SPAN
COLD = NCTX * CAP
EXTRA = NCTX * (SLOT - CAP)
TILE = 64
VM = pl.BlockSpec(memory_space=pltpu.VMEM)
ANY = pl.BlockSpec(memory_space=pl.ANY)


def room(mib):
    return pltpu.CompilerParams(vmem_limit_bytes=mib * 1024 * 1024)


def place(xl, z, c):
    return xl * 2 * Z + z * 2 + c


def z_step(core, i):
    return i + 1 if core == 0 else -i


def z_shift(i):
    return [
        (place(xl, z, c), place(xl, (z + z_step(c, i)) % Z, c))
        for xl in range(2)
        for z in range(Z)
        for c in range(2)
    ]


CORE_PAIRS = [(i, i ^ 1) for i in range(NCTX)]
XLO_PAIRS = [(i, i ^ (2 * Z)) for i in range(NCTX)]
ORDER = (3, 2, 1, 0)


def prepare_kernel(my, keys, values, keys2, values2, id_line, kv, own, alone, sem):
    loads = [
        pltpu.make_async_copy(keys, kv.at[:TOK, :HD], sem.at[0]),
        pltpu.make_async_copy(values, kv.at[:TOK, HD:], sem.at[1]),
    ]
    for load in loads:
        load.start()
    kv[TOK:, :HD] = keys2[...]
    kv[TOK:, HD:] = values2[...]
    expert = lax.broadcasted_iota(jnp.int32, (NCTX, TOK), 0)
    named = (expert == id_line[0:1, :]).astype(F32) + (expert == id_line[1:2, :]).astype(F32)
    hot = (jnp.sum(named, axis=1, keepdims=True) > CAP).astype(jnp.int32)
    place_of = lax.broadcasted_iota(jnp.int32, (NCTX, 1), 0)
    own[0] = jnp.sum(hot * (place_of == my[0]).astype(jnp.int32))
    chip = hot * (place_of >> 1)
    low = jnp.max(chip + (1 - hot) * -1)
    high = jnp.min(chip + (1 - hot) * NCTX)
    alone[0] = (low == high).astype(jnp.int32)
    for load in loads:
        load.wait()


def prepare(my, keys, values, keys2, values2, id_line):
    return pl.pallas_call(
        prepare_kernel,
        name="prepare",
        out_shape=(
            jax.ShapeDtypeStruct((2 * TOK, 2 * HD), BF),
            jax.ShapeDtypeStruct((1,), jnp.int32),
            jax.ShapeDtypeStruct((1,), jnp.int32),
        ),
        in_specs=[pl.BlockSpec(memory_space=pltpu.SMEM), ANY, ANY] + [VM] * 3,
        out_specs=(VM,) + (pl.BlockSpec(memory_space=pltpu.SMEM),) * 2,
        scratch_shapes=[pltpu.SemaphoreType.DMA((2,))],
        compiler_params=room(8),
    )(my, keys, values, keys2, values2, id_line)


def join_kernel(*refs):
    out = refs[-1]
    for b, ref in enumerate(refs[:-1]):
        out[b * 2 * TOK : (b + 1) * 2 * TOK] = ref[...]


def join(blocks):
    return pl.pallas_call(
        join_kernel,
        name="join",
        out_shape=jax.ShapeDtypeStruct((len(blocks) * 2 * TOK, 2 * HD), BF),
        in_specs=[VM] * len(blocks),
        out_specs=VM,
        compiler_params=room(6),
    )(*blocks)


def join_near_kernel(q, *refs):
    out, q6, sem = refs[-3:]
    loads = [
        pltpu.make_async_copy(
            q.at[:, h * HD : (h + 1) * HD], q6.at[h * TOK : (h + 1) * TOK], sem.at[h]
        )
        for h in range(6)
    ]
    for load in loads:
        load.start()
    join_kernel(*refs[:-2])
    for load in loads:
        load.wait()


def join_near(q, blocks):
    return pl.pallas_call(
        join_near_kernel,
        name="join_near",
        out_shape=(
            jax.ShapeDtypeStruct((len(blocks) * 2 * TOK, 2 * HD), BF),
            jax.ShapeDtypeStruct((6 * TOK, HD), BF),
        ),
        in_specs=[ANY] + [VM] * len(blocks),
        out_specs=(VM, VM),
        scratch_shapes=[pltpu.SemaphoreType.DMA((6,))],
        compiler_params=room(6),
    )(q, *blocks)


def gather_kv(kv, q):
    near = [lax.ppermute(kv, "ctx", z_shift(i)) for i in ORDER]
    far = [lax.ppermute(block, "ctx", XLO_PAIRS) for block in near]
    ka, q6 = join_near(q, near)
    kb = join(far)
    kc, kd = [lax.ppermute(part, "ctx", CORE_PAIRS) for part in (ka, kb)]
    return ka, kb, kc, kd, q6


def column(line):
    return jnp.transpose(jnp.broadcast_to(line.astype(F32), (TOK, TOK)))[:, 0:1]


def ranks(id_line, axis):
    a = lax.broadcasted_iota(jnp.int32, (TOK, TOK), axis)
    b = lax.broadcasted_iota(jnp.int32, (TOK, TOK), 1 - axis)
    before = a < b
    line0, line1 = id_line[0:1, :].astype(F32), id_line[1:2, :].astype(F32)
    col0, col1 = column(line0), column(line1)
    if axis == 0:
        own0, own1, oth0, oth1 = line0, line1, col0, col1
    else:
        own0, own1, oth0, oth1 = col0, col1, line0, line1

    def count(mask):
        return jnp.sum(mask.astype(F32), axis=axis, keepdims=True).astype(jnp.int32)

    rank0 = count((oth0 == own0) & before)
    rank1 = count(oth0 == own1) + count((oth1 == own1) & before)
    return own0.astype(jnp.int32), own1.astype(jnp.int32), rank0, rank1


def split_row(expert, rank):
    over = (rank >= SLOT).astype(jnp.int32)
    return (expert ^ over) * SPAN + rank - (SLOT - CAP) * over


def slot_map(c, extra, transposed):
    count = SLOT - CAP if extra else CAP
    rows, cols = 8 * count, 8 * SPAN
    shape = (cols, rows) if transposed else (rows, cols)
    i = lax.broadcasted_iota(jnp.int32, shape, 1 if transposed else 0)
    j = lax.broadcasted_iota(jnp.int32, shape, 0 if transposed else 1)
    source = (i * (43 if count == CAP else 86)) >> 9
    slot = i - source * count + (CAP if extra else 0)
    return (j == source * SPAN + c * SLOT + slot).astype(F32).astype(BF)


def place_kernel(att, id_line, placed):
    id0, id1, r0, r1 = ranks(id_line, 0)
    slot = lax.broadcasted_iota(jnp.int32, (NCTX * SLOTS, TOK), 0)
    pick = (slot == id0 * SLOTS + r0) | (slot == id1 * SLOTS + r1)
    pick = pick.astype(F32).astype(BF)
    placed[...] = jnp.dot(pick, att[...], preferred_element_type=F32).astype(BF)


def attend_kernel(
    my_ref, q6, ka, kb, kc, kd, id_line, att, placed, s, m, total, acc, meta
):
    my = my_ref[0]
    xl, z, core = my // (2 * Z), (my // 2) % Z, my % 2
    at = 0
    for cc in (core, 1 - core):
        for xx in (xl, 1 - xl):
            for i in ORDER:
                step = jnp.where(cc == 0, i + 1, -i)
                for which in (cc, 1 - cc):
                    meta[at] = (place(xx, (z + Z - step) % Z, which) - my) * TOK
                    at += 1
    m[...] = jnp.full_like(m, NEG)
    gap = (lax.broadcasted_iota(jnp.int32, (6 * TOK, TOK), 0) & (TOK - 1)) - lax.broadcasted_iota(
        jnp.int32, (6 * TOK, TOK), 1
    )
    scale = HD ** (-0.5) * LOG2E
    quarter = NCTX // 4 * TOK
    wide = BLOCKS * TOK
    for side, kv in enumerate((ka, kb, kc, kd)):

        def scores(i, carry):
            rows = pl.ds(pl.multiple_of(i * wide, wide), wide)
            cols = pl.ds(pl.multiple_of(side * quarter + i * wide, wide), wide)
            value = lax.dot_general(
                q6[...], kv[rows, 0:HD], (((1,), (1,)), ((), ())), preferred_element_type=F32
            )
            base = side * (NCTX // 4) + i * BLOCKS
            pieces = [
                jnp.where(gap >= meta[base + b], value[:, b * TOK : (b + 1) * TOK], NEG)
                for b in range(BLOCKS)
            ]
            s[:, cols] = jnp.concatenate(pieces, axis=1)
            m[...] = jnp.maximum(m[...], functools.reduce(jnp.maximum, pieces))
            return carry

        lax.fori_loop(0, NCTX // 4 // BLOCKS, scores, 0)
    top = jnp.broadcast_to(jnp.max(m[...], axis=1, keepdims=True), (6 * TOK, TOK))
    m[...] = top
    total[...] = jnp.zeros_like(total)
    acc[...] = jnp.zeros_like(acc)
    for side, kv in enumerate((ka, kb, kc, kd)):

        def mix(i, carry):
            rows = pl.ds(pl.multiple_of(i * wide, wide), wide)
            cols = pl.ds(pl.multiple_of(side * quarter + i * wide, wide), wide)
            part = s[:, cols]
            top = m[...]
            pieces = [
                jnp.exp2((part[:, b * TOK : (b + 1) * TOK] - top) * scale) for b in range(BLOCKS)
            ]
            total[...] += functools.reduce(jnp.add, pieces)
            p = jnp.concatenate([piece.astype(BF) for piece in pieces], axis=1)
            acc[...] += jnp.dot(p, kv[rows, HD:], preferred_element_type=F32)
            return carry

        lax.fori_loop(0, NCTX // 4 // BLOCKS, mix, 0)
    out = (acc[...] / jnp.sum(total[...], axis=1, keepdims=True)).astype(BF)
    for h in range(6):
        att[:, h * HD : (h + 1) * HD] = out[h * TOK : (h + 1) * TOK]
    id0, id1, r0, r1 = ranks(id_line, 0)
    slot = lax.broadcasted_iota(jnp.int32, (ROWS, TOK), 0)
    row0, row1 = split_row(id0, r0), split_row(id1, r1)
    filled = jnp.zeros((ROWS, THIRD), F32)
    for c in range(3):
        pick = (slot == row0 + c * SLOT) | (slot == row1 + c * SLOT)
        pick = pick.astype(F32).astype(BF)
        filled += jnp.dot(pick, att[:, c * THIRD : (c + 1) * THIRD], preferred_element_type=F32)
    placed[...] = filled.astype(BF)


def attend(my, q, ka, kb, kc, kd, id_line):
    return pl.pallas_call(
        attend_kernel,
        name="attend",
        out_shape=(
            jax.ShapeDtypeStruct((TOK, 6 * HD), BF),
            jax.ShapeDtypeStruct((ROWS, THIRD), BF),
        ),
        in_specs=[pl.BlockSpec(memory_space=pltpu.SMEM)] + [VM] * 6,
        out_specs=(VM, VM),
        scratch_shapes=[
            pltpu.VMEM((6 * TOK, NCTX * TOK), F32),
            pltpu.VMEM((6 * TOK, TOK), F32),
            pltpu.VMEM((6 * TOK, TOK), F32),
            pltpu.VMEM((6 * TOK, HD), F32),
            pltpu.SMEM((NCTX,), jnp.int32),
        ],
        compiler_params=room(28),
    )(my, q, ka, kb, kc, kd, id_line)


def gate_up_kernel(x, wg, wu, out):
    width = wg.shape[2]
    out[0, :, :width] = jnp.dot(x[...], wg[0], preferred_element_type=F32).astype(BF)
    out[0, :, width:] = jnp.dot(x[...], wu[0], preferred_element_type=F32).astype(BF)


def gate_up(x, wg, wu):
    rows, depth = x.shape
    width = wg.shape[2] // NEP
    weight = pl.BlockSpec((1, depth, width), lambda j: (0, 0, j))
    return pl.pallas_call(
        gate_up_kernel,
        name="gate_up",
        grid=(NEP,),
        out_shape=jax.ShapeDtypeStruct((NEP, rows, 2 * width), BF),
        in_specs=[pl.BlockSpec((rows, depth), lambda j: (0, 0)), weight, weight],
        out_specs=pl.BlockSpec((1, rows, 2 * width), lambda j: (j, 0, 0)),
        compiler_params=room(24),
    )(x, wg, wu)


def hidden_kernel(parts, out):
    width = out.shape[2]
    total = parts[0].astype(F32)
    for j in range(1, NEP):
        total += parts[j].astype(F32)
    gate, up = total[:, :width], total[:, width:]
    value = (gate / (1.0 + jnp.exp(-gate)) * up).astype(BF)
    for j in range(NEP):
        out[j] = value


def hidden(parts):
    _, rows, width = parts.shape
    tile = TILE if rows % 192 else 192
    return pl.pallas_call(
        hidden_kernel,
        name="hidden",
        grid=(rows // tile,),
        out_shape=jax.ShapeDtypeStruct((NEP, rows, width // 2), BF),
        in_specs=[pl.BlockSpec((NEP, tile, width), lambda i: (0, i, 0))],
        out_specs=pl.BlockSpec((NEP, tile, width // 2), lambda i: (0, i, 0)),
        compiler_params=room(12),
    )(parts)


def down_kernel(h, w, out, acc):
    j = pl.program_id(0)
    part = jnp.dot(h[0], w[0], preferred_element_type=F32)

    @pl.when(j == 0)
    def _():
        acc[...] = part

    @pl.when(j > 0)
    def _():
        acc[...] += part

    @pl.when(j == NEP - 1)
    def _():
        out[...] = acc[...].astype(BF)


def down(h, w):
    _, rows, width = h.shape
    cols = w.shape[2]
    return pl.pallas_call(
        down_kernel,
        name="down",
        grid=(NEP,),
        out_shape=jax.ShapeDtypeStruct((rows, cols), BF),
        in_specs=[
            pl.BlockSpec((1, rows, width), lambda j: (j, 0, 0)),
            pl.BlockSpec((1, width, cols), lambda j: (0, j, 0)),
        ],
        out_specs=pl.BlockSpec((rows, cols), lambda j: (0, 0)),
        scratch_shapes=[pltpu.VMEM((rows, cols), F32)],
        compiler_params=room(16),
    )(h, w)


def split_gate_up_kernel(own, arr, wg, wu, sg, su, out, x, bg, bu, cg, cu, sem):
    loads = [
        pltpu.make_async_copy(wg.at[0], bg, sem.at[0]),
        pltpu.make_async_copy(wu.at[0], bu, sem.at[1]),
        pltpu.make_async_copy(sg.at[0], cg, sem.at[2]),
        pltpu.make_async_copy(su.at[0], cu, sem.at[3]),
    ]
    for load in loads[:2]:
        load.start()
    width = wg.shape[2] // NEP
    n, m = 8 * CAP, 8 * (SLOT - CAP)
    for c in range(3):
        cols = slice(c * THIRD, (c + 1) * THIRD)
        cold, extra = slot_map(c, False, False), slot_map(c, True, False)
        for g in range(NCTX // 8):
            group = arr[g * 8 * SPAN : (g + 1) * 8 * SPAN]
            x[g * n : (g + 1) * n, cols] = jnp.dot(
                cold, group, preferred_element_type=F32
            ).astype(BF)
            x[COLD + g * m : COLD + (g + 1) * m, cols] = jnp.dot(
                extra, group, preferred_element_type=F32
            ).astype(BF)

    def piece(lo, hi, at, w):
        for j in range(NEP):
            out[j, lo:hi, at : at + width] = jnp.dot(
                x[lo:hi], w[:, j * width : (j + 1) * width], preferred_element_type=F32
            ).astype(BF)

    loads[0].wait()
    loads[2].start()
    piece(0, COLD, 0, bg)
    loads[1].wait()
    loads[3].start()
    piece(0, COLD, width, bu)
    loads[2].wait()
    loads[3].wait()

    @pl.when(own[0] == 1)
    def _():
        piece(COLD, COLD + EXTRA, 0, bg)
        piece(COLD, COLD + EXTRA, width, bu)

    @pl.when(own[0] == 0)
    def _():
        piece(COLD, COLD + EXTRA, 0, cg)
        piece(COLD, COLD + EXTRA, width, cu)


def split_gate_up(own, arr, wg, wu, sg, su):
    _, depth, full = wg.shape
    rows = COLD + EXTRA
    return pl.pallas_call(
        split_gate_up_kernel,
        name="split_gate_up",
        out_shape=jax.ShapeDtypeStruct((NEP, rows, 2 * full // NEP), BF),
        in_specs=[pl.BlockSpec(memory_space=pltpu.SMEM), VM, ANY, ANY, ANY, ANY],
        out_specs=VM,
        scratch_shapes=[
            pltpu.VMEM((rows, depth), BF),
            pltpu.VMEM((depth, full), BF),
            pltpu.VMEM((depth, full), BF),
            pltpu.VMEM((depth, full), BF),
            pltpu.VMEM((depth, full), BF),
            pltpu.SemaphoreType.DMA((4,)),
        ],
        compiler_params=room(26),
    )(own, arr, wg, wu, sg, su)


def split_down_kernel(own, h, w, v, out, wide, y, theirs, sem):
    load = pltpu.make_async_copy(v, theirs, sem)
    load.start()
    width = h.shape[2]
    for j in range(NEP):
        wide[:, j * width : (j + 1) * width] = h[j]

    def product(lo, hi, weights):
        for c in range(3):
            cols = slice(c * THIRD, (c + 1) * THIRD)
            y[lo:hi, cols] = jnp.dot(
                wide[lo:hi], weights[0, :, cols], preferred_element_type=F32
            ).astype(BF)

    product(0, COLD, w)
    load.wait()

    @pl.when(own[0] == 1)
    def _():
        product(COLD, COLD + EXTRA, w)

    @pl.when(own[0] == 0)
    def _():
        product(COLD, COLD + EXTRA, theirs)

    n, m = 8 * CAP, 8 * (SLOT - CAP)
    maps = [(slot_map(c, False, True), slot_map(c, True, True)) for c in range(3)]
    for g in range(NCTX // 8):
        total = jnp.zeros((8 * SPAN, THIRD), F32)
        for c in range(3):
            cols = slice(c * THIRD, (c + 1) * THIRD)
            cold, extra = maps[c]
            total += jnp.dot(cold, y[g * n : (g + 1) * n, cols], preferred_element_type=F32)
            total += jnp.dot(
                extra, y[COLD + g * m : COLD + (g + 1) * m, cols], preferred_element_type=F32
            )
        out[g * 8 * SPAN : (g + 1) * 8 * SPAN] = total.astype(BF)


def split_down(own, h, w, v):
    _, rows, width = h.shape
    _, depth, cols = w.shape
    return pl.pallas_call(
        split_down_kernel,
        name="split_down",
        out_shape=jax.ShapeDtypeStruct((ROWS, THIRD), BF),
        in_specs=[pl.BlockSpec(memory_space=pltpu.SMEM), VM, VM, ANY],
        out_specs=VM,
        scratch_shapes=[
            pltpu.VMEM((rows, depth), BF),
            pltpu.VMEM((rows, cols), BF),
            pltpu.VMEM(v.shape, BF),
            pltpu.SemaphoreType.DMA,
        ],
        compiler_params=room(20),
    )(own, h, w, v)


def shares(logits):
    l0, l1 = column(logits[0:1, :]), column(logits[1:2, :])
    top = jnp.maximum(l0, l1)
    e0, e1 = jnp.exp(l0 - top), jnp.exp(l1 - top)
    both = e0 + e1
    return e0 / both, e1 / both


def split_combine_kernel(answers, att, logits, id_line, out):
    id0, id1, r0, r1 = ranks(id_line, 1)
    slot = lax.broadcasted_iota(jnp.int32, (TOK, ROWS), 1)
    row0, row1 = split_row(id0, r0), split_row(id1, r1)
    s0, s1 = shares(logits)
    for c in range(3):
        cols = slice(c * THIRD, (c + 1) * THIRD)
        pick0 = (slot == row0 + c * SLOT).astype(F32).astype(BF)
        pick1 = (slot == row1 + c * SLOT).astype(F32).astype(BF)
        first = jnp.dot(pick0, answers[...], preferred_element_type=F32)
        second = jnp.dot(pick1, answers[...], preferred_element_type=F32)
        out[:, cols] = (att[:, cols].astype(F32) + first * s0 + second * s1).astype(BF)


def combine_kernel(answers, att, logits, id_line, out):
    id0, id1, r0, r1 = ranks(id_line, 1)
    slot = lax.broadcasted_iota(jnp.int32, (TOK, NCTX * SLOTS), 1)
    pick0 = (slot == id0 * SLOTS + r0).astype(F32).astype(BF)
    pick1 = (slot == id1 * SLOTS + r1).astype(F32).astype(BF)
    s0, s1 = shares(logits)
    first = jnp.dot(pick0, answers[...], preferred_element_type=F32) * s0
    second = jnp.dot(pick1, answers[...], preferred_element_type=F32) * s1
    out[...] = (att[...].astype(F32) + first + second).astype(BF)


def place_rows(att, id_line):
    return pl.pallas_call(
        place_kernel,
        name="place_rows",
        out_shape=jax.ShapeDtypeStruct((NCTX * SLOTS, att.shape[1]), BF),
        in_specs=[VM] * 2,
        out_specs=VM,
        compiler_params=room(8),
    )(att, id_line)


def combine(kernel, answers, att, logits, id_line):
    return pl.pallas_call(
        kernel,
        name="combine",
        out_shape=jax.ShapeDtypeStruct(att.shape, BF),
        in_specs=[VM] * 4,
        out_specs=VM,
        compiler_params=room(10),
    )(answers, att, logits, id_line)


def swap(x, axis):
    return lax.all_to_all(x, axis, 0, 0, tiled=True)


def owners_only(args):
    att, _, gate_weight, up_weight, down_weight, _, _, _, _, id_line, logits = args
    outgoing = place_rows(att, id_line).reshape(NCTX, SLOTS, att.shape[1])
    arrived = swap(outgoing, "ctx")
    parts = swap(gate_up(arrived.reshape(NCTX * SLOTS, -1), gate_weight, up_weight), "ep")
    produced = down(swap(hidden(parts), "ep"), down_weight)
    back = swap(produced.reshape(NCTX, SLOTS, -1), "ctx")
    return combine(combine_kernel, back.reshape(NCTX * SLOTS, -1), att, logits, id_line)


def both_cores(args):
    att, placed, wg, wu, wd, sg, su, sd, own, id_line, logits = args
    arrived = swap(placed.reshape(NCTX, SPAN, THIRD), "ctx").reshape(ROWS, THIRD)
    parts = swap(split_gate_up(own, arrived, wg, wu, sg, su), "ep")
    produced = split_down(own, swap(hidden(parts), "ep"), wd, sd)
    back = swap(produced.reshape(NCTX, SPAN, THIRD), "ctx").reshape(ROWS, THIRD)
    return combine(split_combine_kernel, back, att, logits, id_line)


def on_device(queries, keys, values, gate_weight, up_weight, down_weight, expert_ids, route_logits):
    my = lax.axis_index("ctx").astype(jnp.int32).reshape(1)
    id_line, logits = expert_ids.T, route_logits.T
    keys2, values2 = [lax.ppermute(a, "ctx", CORE_PAIRS) for a in (keys, values)]
    kv, own, one_chip = prepare(my, keys, values, keys2, values2, id_line)
    weights = (gate_weight, up_weight, down_weight)
    held = lax.optimization_barrier((kv,) + weights)
    theirs = [lax.ppermute(w, "ctx", CORE_PAIRS) for w in held[1:]]
    ka, kb, kc, kd, q6 = gather_kv(kv, queries)
    att, placed = attend(my, q6, ka, kb, kc, kd, id_line)
    args = (att, placed, *weights, *theirs, own, id_line, logits)
    return lax.cond(one_chip[0] == 1, owners_only, both_cores, args)


def solution(mesh):
    in_specs = (
        P("ctx", "ep"),
        P("ctx", "ep"),
        P("ctx", "ep"),
        P("ctx", "ep", None),
        P("ctx", "ep", None),
        P("ctx", None, "ep"),
        P("ctx", None),
        P("ctx", None),
    )
    return jax.shard_map(
        on_device, mesh=mesh, in_specs=in_specs, out_specs=P("ctx", "ep"), check_vma=False
    )
```

```python
import functools

import jax
import jax.numpy as jnp
from jax import lax
from jax.experimental import pallas as pl
from jax.experimental.pallas import tpu as pltpu
from jax.sharding import PartitionSpec as P


BF = jnp.bfloat16
F32 = jnp.float32
H = 48
KVH = 8
HD = 128
TOK = 128
NCTX = 32
NEP = 8
SLOTS = 24
Z = 8
NEG = -1e30
LOG2E = 1.4426950408889634
BLOCKS = 4
CAP = 12
THIRD = 256
SLOT = 18
SPAN = 56
ROWS = NCTX * SPAN
COLD = NCTX * CAP
EXTRA = NCTX * (SLOT - CAP)
TILE = 64
NY = NEP // 2
HALF = (COLD + EXTRA) // 2
VM = pl.BlockSpec(memory_space=pltpu.VMEM)
ANY = pl.BlockSpec(memory_space=pl.ANY)
HBM = pl.BlockSpec(memory_space=pltpu.HBM)
SM = pl.BlockSpec(memory_space=pltpu.SMEM)


def hold(x):
    return pltpu.with_memory_space_constraint(x, pltpu.HBM)


def room(mib):
    return pltpu.CompilerParams(vmem_limit_bytes=mib * 1024 * 1024)


def place(xl, z, c):
    return xl * 2 * Z + z * 2 + c


def z_step(core, i):
    return i + 1 if core == 0 else -i


def z_shift(i):
    return [
        (place(xl, z, c), place(xl, (z + z_step(c, i)) % Z, c))
        for xl in range(2)
        for z in range(Z)
        for c in range(2)
    ]


X_PAIRS = [(i, i ^ 1) for i in range(NEP)]
Y_GROUPS = [[2 * y + x for y in range(NEP // 2)] for x in range(2)]
CORE_PAIRS = [(i, i ^ 1) for i in range(NCTX)]
XLO_PAIRS = [(i, i ^ (2 * Z)) for i in range(NCTX)]
ORDER = (3, 2, 1, 0)


def prepare_kernel(my, keys, values, keys2, values2, id_line, kv, own, alone, sem):
    loads = [
        pltpu.make_async_copy(keys, kv.at[:TOK, :HD], sem.at[0]),
        pltpu.make_async_copy(values, kv.at[:TOK, HD:], sem.at[1]),
    ]
    for load in loads:
        load.start()
    kv[TOK:, :HD] = keys2[...]
    kv[TOK:, HD:] = values2[...]
    expert = lax.broadcasted_iota(jnp.int32, (NCTX, TOK), 0)
    named = (expert == id_line[0:1, :]).astype(F32) + (expert == id_line[1:2, :]).astype(F32)
    hot = (jnp.sum(named, axis=1, keepdims=True) > CAP).astype(jnp.int32)
    place_of = lax.broadcasted_iota(jnp.int32, (NCTX, 1), 0)
    own[0] = jnp.sum(hot * (place_of == my[0]).astype(jnp.int32))
    chip = hot * (place_of >> 1)
    low = jnp.max(chip + (1 - hot) * -1)
    high = jnp.min(chip + (1 - hot) * NCTX)
    alone[0] = (low == high).astype(jnp.int32)
    for load in loads:
        load.wait()


def prepare(my, keys, values, keys2, values2, id_line):
    keys, values = hold(keys), hold(values)
    return pl.pallas_call(
        prepare_kernel,
        name="prepare",
        out_shape=(
            jax.ShapeDtypeStruct((2 * TOK, 2 * HD), BF),
            jax.ShapeDtypeStruct((1,), jnp.int32),
            jax.ShapeDtypeStruct((1,), jnp.int32),
        ),
        in_specs=[SM, HBM, HBM] + [VM] * 3,
        out_specs=(VM,) + (pl.BlockSpec(memory_space=pltpu.SMEM),) * 2,
        scratch_shapes=[pltpu.SemaphoreType.DMA((2,))],
        compiler_params=room(8),
    )(my, keys, values, keys2, values2, id_line)


def join_kernel(*refs):
    out = refs[-1]
    for b, ref in enumerate(refs[:-1]):
        out[b * 2 * TOK : (b + 1) * 2 * TOK] = ref[...]


def join(blocks):
    return pl.pallas_call(
        join_kernel,
        name="join",
        out_shape=jax.ShapeDtypeStruct((len(blocks) * 2 * TOK, 2 * HD), BF),
        in_specs=[VM] * len(blocks),
        out_specs=VM,
        compiler_params=room(6),
    )(*blocks)


def join_near_kernel(q, *refs):
    out, q6, sem = refs[-3:]
    loads = [
        pltpu.make_async_copy(
            q.at[:, h * HD : (h + 1) * HD], q6.at[h * TOK : (h + 1) * TOK], sem.at[h]
        )
        for h in range(6)
    ]
    for load in loads:
        load.start()
    join_kernel(*refs[:-2])
    for load in loads:
        load.wait()


def join_near(q, blocks):
    q = hold(q)
    return pl.pallas_call(
        join_near_kernel,
        name="join_near",
        out_shape=(
            jax.ShapeDtypeStruct((len(blocks) * 2 * TOK, 2 * HD), BF),
            jax.ShapeDtypeStruct((6 * TOK, HD), BF),
        ),
        in_specs=[HBM] + [VM] * len(blocks),
        out_specs=(VM, VM),
        scratch_shapes=[pltpu.SemaphoreType.DMA((6,))],
        compiler_params=room(6),
    )(q, *blocks)


def gather_kv(kv, q):
    near = [lax.ppermute(kv, "ctx", z_shift(i)) for i in ORDER]
    far = [lax.ppermute(block, "ctx", XLO_PAIRS) for block in near]
    ka, q6 = join_near(q, near)
    kb = join(far)
    kc, kd = [lax.ppermute(part, "ctx", CORE_PAIRS) for part in (ka, kb)]
    return ka, kb, kc, kd, q6


def column(line):
    return jnp.transpose(jnp.broadcast_to(line.astype(F32), (TOK, TOK)))[:, 0:1]


def ranks(id_line, axis):
    a = lax.broadcasted_iota(jnp.int32, (TOK, TOK), axis)
    b = lax.broadcasted_iota(jnp.int32, (TOK, TOK), 1 - axis)
    before = a < b
    line0, line1 = id_line[0:1, :].astype(F32), id_line[1:2, :].astype(F32)
    col0, col1 = column(line0), column(line1)
    if axis == 0:
        own0, own1, oth0, oth1 = line0, line1, col0, col1
    else:
        own0, own1, oth0, oth1 = col0, col1, line0, line1

    def count(mask):
        return jnp.sum(mask.astype(F32), axis=axis, keepdims=True).astype(jnp.int32)

    rank0 = count((oth0 == own0) & before)
    rank1 = count(oth0 == own1) + count((oth1 == own1) & before)
    return own0.astype(jnp.int32), own1.astype(jnp.int32), rank0, rank1


def split_row(expert, rank):
    over = (rank >= SLOT).astype(jnp.int32)
    return (expert ^ over) * SPAN + rank - (SLOT - CAP) * over


def slot_map(c, extra, transposed):
    count = SLOT - CAP if extra else CAP
    rows, cols = 8 * count, 8 * SPAN
    shape = (cols, rows) if transposed else (rows, cols)
    i = lax.broadcasted_iota(jnp.int32, shape, 1 if transposed else 0)
    j = lax.broadcasted_iota(jnp.int32, shape, 0 if transposed else 1)
    source = (i * (43 if count == CAP else 86)) >> 9
    slot = i - source * count + (CAP if extra else 0)
    return (j == source * SPAN + c * SLOT + slot).astype(F32).astype(BF)


def place_kernel(att, id_line, placed):
    id0, id1, r0, r1 = ranks(id_line, 0)
    slot = lax.broadcasted_iota(jnp.int32, (NCTX * SLOTS, TOK), 0)
    pick = (slot == id0 * SLOTS + r0) | (slot == id1 * SLOTS + r1)
    pick = pick.astype(F32).astype(BF)
    placed[...] = jnp.dot(pick, att[...], preferred_element_type=F32).astype(BF)


def attend_kernel(
    my_ref, q6, ka, kb, kc, kd, id_line, att, placed, s, m, total, acc, meta
):
    my = my_ref[0]
    xl, z, core = my // (2 * Z), (my // 2) % Z, my % 2
    at = 0
    for cc in (core, 1 - core):
        for xx in (xl, 1 - xl):
            for i in ORDER:
                step = jnp.where(cc == 0, i + 1, -i)
                for which in (cc, 1 - cc):
                    meta[at] = (place(xx, (z + Z - step) % Z, which) - my) * TOK
                    at += 1
    m[...] = jnp.full_like(m, NEG)
    gap = (lax.broadcasted_iota(jnp.int32, (6 * TOK, TOK), 0) & (TOK - 1)) - lax.broadcasted_iota(
        jnp.int32, (6 * TOK, TOK), 1
    )
    scale = HD ** (-0.5) * LOG2E
    quarter = NCTX // 4 * TOK
    wide = BLOCKS * TOK
    for side, kv in enumerate((ka, kb, kc, kd)):

        def scores(i, carry):
            rows = pl.ds(pl.multiple_of(i * wide, wide), wide)
            cols = pl.ds(pl.multiple_of(side * quarter + i * wide, wide), wide)
            value = lax.dot_general(
                q6[...], kv[rows, 0:HD], (((1,), (1,)), ((), ())), preferred_element_type=F32
            )
            base = side * (NCTX // 4) + i * BLOCKS
            pieces = [
                jnp.where(gap >= meta[base + b], value[:, b * TOK : (b + 1) * TOK], NEG)
                for b in range(BLOCKS)
            ]
            s[:, cols] = jnp.concatenate(pieces, axis=1)
            m[...] = jnp.maximum(m[...], functools.reduce(jnp.maximum, pieces))
            return carry

        lax.fori_loop(0, NCTX // 4 // BLOCKS, scores, 0)
    top = jnp.broadcast_to(jnp.max(m[...], axis=1, keepdims=True), (6 * TOK, TOK))
    m[...] = top
    total[...] = jnp.zeros_like(total)
    acc[...] = jnp.zeros_like(acc)
    for side, kv in enumerate((ka, kb, kc, kd)):

        def mix(i, carry):
            rows = pl.ds(pl.multiple_of(i * wide, wide), wide)
            cols = pl.ds(pl.multiple_of(side * quarter + i * wide, wide), wide)
            part = s[:, cols]
            top = m[...]
            pieces = [
                jnp.exp2((part[:, b * TOK : (b + 1) * TOK] - top) * scale) for b in range(BLOCKS)
            ]
            total[...] += functools.reduce(jnp.add, pieces)
            p = jnp.concatenate([piece.astype(BF) for piece in pieces], axis=1)
            acc[...] += jnp.dot(p, kv[rows, HD:], preferred_element_type=F32)
            return carry

        lax.fori_loop(0, NCTX // 4 // BLOCKS, mix, 0)
    out = (acc[...] / jnp.sum(total[...], axis=1, keepdims=True)).astype(BF)
    for h in range(6):
        att[:, h * HD : (h + 1) * HD] = out[h * TOK : (h + 1) * TOK]
    id0, id1, r0, r1 = ranks(id_line, 0)
    slot = lax.broadcasted_iota(jnp.int32, (ROWS, TOK), 0)
    row0, row1 = split_row(id0, r0), split_row(id1, r1)
    filled = jnp.zeros((ROWS, THIRD), F32)
    for c in range(3):
        pick = (slot == row0 + c * SLOT) | (slot == row1 + c * SLOT)
        pick = pick.astype(F32).astype(BF)
        filled += jnp.dot(pick, att[:, c * THIRD : (c + 1) * THIRD], preferred_element_type=F32)
    placed[...] = filled.astype(BF)


def attend(my, q, ka, kb, kc, kd, id_line):
    return pl.pallas_call(
        attend_kernel,
        name="attend",
        out_shape=(
            jax.ShapeDtypeStruct((TOK, 6 * HD), BF),
            jax.ShapeDtypeStruct((ROWS, THIRD), BF),
        ),
        in_specs=[pl.BlockSpec(memory_space=pltpu.SMEM)] + [VM] * 6,
        out_specs=(VM, VM),
        scratch_shapes=[
            pltpu.VMEM((6 * TOK, NCTX * TOK), F32),
            pltpu.VMEM((6 * TOK, TOK), F32),
            pltpu.VMEM((6 * TOK, TOK), F32),
            pltpu.VMEM((6 * TOK, HD), F32),
            pltpu.SMEM((NCTX,), jnp.int32),
        ],
        compiler_params=room(28),
    )(my, q, ka, kb, kc, kd, id_line)


def gate_up_kernel(x, wg, wu, out):
    width = wg.shape[2]
    out[0, :, :width] = jnp.dot(x[...], wg[0], preferred_element_type=F32).astype(BF)
    out[0, :, width:] = jnp.dot(x[...], wu[0], preferred_element_type=F32).astype(BF)


def gate_up(x, wg, wu):
    rows, depth = x.shape
    width = wg.shape[2] // NEP
    weight = pl.BlockSpec((1, depth, width), lambda j: (0, 0, j))
    return pl.pallas_call(
        gate_up_kernel,
        name="gate_up",
        grid=(NEP,),
        out_shape=jax.ShapeDtypeStruct((NEP, rows, 2 * width), BF),
        in_specs=[pl.BlockSpec((rows, depth), lambda j: (0, 0)), weight, weight],
        out_specs=pl.BlockSpec((1, rows, 2 * width), lambda j: (j, 0, 0)),
        compiler_params=room(24),
    )(x, wg, wu)


def hidden_kernel(parts, out):
    width = out.shape[2]
    total = parts[0].astype(F32)
    for j in range(1, NEP):
        total += parts[j].astype(F32)
    gate, up = total[:, :width], total[:, width:]
    value = (gate / (1.0 + jnp.exp(-gate)) * up).astype(BF)
    for j in range(NEP):
        out[j] = value


def hidden(parts):
    _, rows, width = parts.shape
    tile = TILE if rows % 192 else 192
    return pl.pallas_call(
        hidden_kernel,
        name="hidden",
        grid=(rows // tile,),
        out_shape=jax.ShapeDtypeStruct((NEP, rows, width // 2), BF),
        in_specs=[pl.BlockSpec((NEP, tile, width), lambda i: (0, i, 0))],
        out_specs=pl.BlockSpec((NEP, tile, width // 2), lambda i: (0, i, 0)),
        compiler_params=room(12),
    )(parts)


def down_kernel(h, w, out, acc):
    j = pl.program_id(0)
    part = jnp.dot(h[0], w[0], preferred_element_type=F32)

    @pl.when(j == 0)
    def _():
        acc[...] = part

    @pl.when(j > 0)
    def _():
        acc[...] += part

    @pl.when(j == NEP - 1)
    def _():
        out[...] = acc[...].astype(BF)


def down(h, w):
    _, rows, width = h.shape
    cols = w.shape[2]
    return pl.pallas_call(
        down_kernel,
        name="down",
        grid=(NEP,),
        out_shape=jax.ShapeDtypeStruct((rows, cols), BF),
        in_specs=[
            pl.BlockSpec((1, rows, width), lambda j: (j, 0, 0)),
            pl.BlockSpec((1, width, cols), lambda j: (0, j, 0)),
        ],
        out_specs=pl.BlockSpec((rows, cols), lambda j: (0, 0)),
        scratch_shapes=[pltpu.VMEM((rows, cols), F32)],
        compiler_params=room(16),
    )(h, w)


def split_gate_up_kernel(
    own, side, arr, wg, wu, sg, su, leave_out, stay_out, cross_out, x, bg, bu, cg, cu,
    leave, stay, cross, sem, done
):
    loads = [
        pltpu.make_async_copy(wg.at[0], bg, sem.at[0]),
        pltpu.make_async_copy(wu.at[0], bu, sem.at[1]),
        pltpu.make_async_copy(sg.at[0], cg, sem.at[2]),
        pltpu.make_async_copy(su.at[0], cu, sem.at[3]),
    ]
    for load in loads[:2]:
        load.start()
    width = wg.shape[2] // NEP
    n, m = 8 * CAP, 8 * (SLOT - CAP)
    for c in range(3):
        cols = slice(c * THIRD, (c + 1) * THIRD)
        cold, extra = slot_map(c, False, False), slot_map(c, True, False)
        for g in range(NCTX // 8):
            group = arr[g * 8 * SPAN : (g + 1) * 8 * SPAN]
            x[g * n : (g + 1) * n, cols] = jnp.dot(
                cold, group, preferred_element_type=F32
            ).astype(BF)
            x[COLD + g * m : COLD + (g + 1) * m, cols] = jnp.dot(
                extra, group, preferred_element_type=F32
            ).astype(BF)

    mine = side[0]

    def cold_piece(at, w):
        for kept, part in ((0, leave), (1, stay)):
            to = mine if kept else 1 - mine
            for y in range(NY):
                cols = pl.ds(pl.multiple_of((2 * y + to) * width, width), width)
                value = jnp.dot(x[:COLD], w[:, cols], preferred_element_type=F32).astype(BF)
                part[y, :, at : at + width] = value[:HALF]
                cross[y, to, : COLD - HALF, at : at + width] = value[HALF:]

    def extra_piece(y, first, second):
        for j in (2 * y, 2 * y + 1):
            for at, w in ((0, first), (width, second)):
                cross[y, j % 2, COLD - HALF :, at : at + width] = jnp.dot(
                    x[COLD:], w[:, j * width : (j + 1) * width], preferred_element_type=F32
                ).astype(BF)

    loads[0].wait()
    loads[2].start()
    cold_piece(0, bg)
    loads[1].wait()
    loads[3].start()
    cold_piece(width, bu)
    stores = [
        pltpu.make_async_copy(leave, leave_out, done.at[0]),
        pltpu.make_async_copy(stay, stay_out, done.at[1]),
    ]
    for store in stores:
        store.start()
    loads[2].wait()
    loads[3].wait()
    for y in range(NY):

        @pl.when(own[0] == 1)
        def _():
            extra_piece(y, bg, bu)

        @pl.when(own[0] == 0)
        def _():
            extra_piece(y, cg, cu)

        store = pltpu.make_async_copy(cross.at[y], cross_out.at[y], done.at[2 + y])
        store.start()
        stores.append(store)
    for store in stores:
        store.wait()


def split_gate_up(own, side, arr, wg, wu, sg, su):
    _, depth, full = wg.shape
    rows = COLD + EXTRA
    return pl.pallas_call(
        split_gate_up_kernel,
        name="split_gate_up",
        out_shape=(
            pltpu.HBM((NY, HALF, 2 * full // NEP), BF),
            pltpu.HBM((NY, HALF, 2 * full // NEP), BF),
            pltpu.HBM((NY, 2, HALF, 2 * full // NEP), BF),
        ),
        in_specs=[SM, SM, VM, ANY, ANY, ANY, ANY],
        out_specs=(HBM, HBM, HBM),
        scratch_shapes=[
            pltpu.VMEM((rows, depth), BF),
            pltpu.VMEM((depth, full), BF),
            pltpu.VMEM((depth, full), BF),
            pltpu.VMEM((depth, full), BF),
            pltpu.VMEM((depth, full), BF),
            pltpu.VMEM((NY, HALF, 2 * full // NEP), BF),
            pltpu.VMEM((NY, HALF, 2 * full // NEP), BF),
            pltpu.VMEM((NY, 2, HALF, 2 * full // NEP), BF),
            pltpu.SemaphoreType.DMA((4,)),
            pltpu.SemaphoreType.DMA((2 + NY,)),
        ],
        compiler_params=room(26),
    )(own, side, arr, wg, wu, sg, su)


def middle_kernel(side, stay, came, cross, onward, leave, keep):
    for y in range(NY):
        onward[y] = (stay[y].astype(F32) + came[y].astype(F32)).astype(BF)
    for to, part in ((1 - side[0], leave), (side[0], keep)):
        total = cross[0, to].astype(F32)
        for y in range(1, NY):
            total += cross[y, to].astype(F32)
        part[...] = total.astype(BF)


def middle(side, stay, came, cross):
    _, rows, width = stay.shape
    tile = rows // 6
    quad = pl.BlockSpec((NY, tile, width), lambda i: (0, i, 0))
    single = pl.BlockSpec((tile, width), lambda i: (i, 0))
    return pl.pallas_call(
        middle_kernel,
        name="middle",
        grid=(6,),
        out_shape=(
            pltpu.HBM(stay.shape, BF),
            pltpu.HBM((rows, width), BF),
            pltpu.HBM((rows, width), BF),
        ),
        in_specs=[SM, quad, quad, pl.BlockSpec((NY, 2, tile, width), lambda i: (0, 0, i, 0))],
        out_specs=(quad, single, single),
        compiler_params=room(24),
    )(side, hold(stay), hold(came), cross)


def split_hidden_kernel(onward, keep, came, out):
    rows, width = keep.shape
    tile = rows // 3
    half = width // 2

    def finish(total, at):
        gate, up = total[:, :half], total[:, half:]
        value = (gate / (1.0 + jnp.exp(-gate)) * up).astype(BF)
        for j in range(NEP):
            out[j, at : at + tile] = value

    for lo in range(0, rows, tile):
        total = onward[0, lo : lo + tile].astype(F32)
        for y in range(1, NY):
            total += onward[y, lo : lo + tile].astype(F32)
        finish(total, lo)
        total = keep[lo : lo + tile].astype(F32) + came[lo : lo + tile].astype(F32)
        finish(total, rows + lo)


def split_hidden(onward, keep, came):
    rows, width = keep.shape
    return pl.pallas_call(
        split_hidden_kernel,
        name="split_hidden",
        out_shape=jax.ShapeDtypeStruct((NEP, 2 * rows, width // 2), BF),
        in_specs=[VM] * 3,
        out_specs=VM,
        compiler_params=room(10),
    )(onward, keep, came)


def split_down_kernel(own, h, w, v, out, wide, y, theirs, sem):
    load = pltpu.make_async_copy(v, theirs, sem)
    load.start()
    width = h.shape[2]
    for j in range(NEP):
        wide[:, j * width : (j + 1) * width] = h[j]

    def product(lo, hi, weights):
        for c in range(3):
            cols = slice(c * THIRD, (c + 1) * THIRD)
            y[lo:hi, cols] = jnp.dot(
                wide[lo:hi], weights[0, :, cols], preferred_element_type=F32
            ).astype(BF)

    product(0, COLD, w)
    load.wait()

    @pl.when(own[0] == 1)
    def _():
        product(COLD, COLD + EXTRA, w)

    @pl.when(own[0] == 0)
    def _():
        product(COLD, COLD + EXTRA, theirs)

    n, m = 8 * CAP, 8 * (SLOT - CAP)
    maps = [(slot_map(c, False, True), slot_map(c, True, True)) for c in range(3)]
    for g in range(NCTX // 8):
        total = jnp.zeros((8 * SPAN, THIRD), F32)
        for c in range(3):
            cols = slice(c * THIRD, (c + 1) * THIRD)
            cold, extra = maps[c]
            total += jnp.dot(cold, y[g * n : (g + 1) * n, cols], preferred_element_type=F32)
            total += jnp.dot(
                extra, y[COLD + g * m : COLD + (g + 1) * m, cols], preferred_element_type=F32
            )
        out[g * 8 * SPAN : (g + 1) * 8 * SPAN] = total.astype(BF)


def split_down(own, h, w, v):
    _, rows, width = h.shape
    _, depth, cols = w.shape
    return pl.pallas_call(
        split_down_kernel,
        name="split_down",
        out_shape=jax.ShapeDtypeStruct((ROWS, THIRD), BF),
        in_specs=[pl.BlockSpec(memory_space=pltpu.SMEM), VM, VM, ANY],
        out_specs=VM,
        scratch_shapes=[
            pltpu.VMEM((rows, depth), BF),
            pltpu.VMEM((rows, cols), BF),
            pltpu.VMEM(v.shape, BF),
            pltpu.SemaphoreType.DMA,
        ],
        compiler_params=room(20),
    )(own, h, w, v)


def shares(logits):
    l0, l1 = column(logits[0:1, :]), column(logits[1:2, :])
    top = jnp.maximum(l0, l1)
    e0, e1 = jnp.exp(l0 - top), jnp.exp(l1 - top)
    both = e0 + e1
    return e0 / both, e1 / both


def split_combine_kernel(answers, att, logits, id_line, out):
    id0, id1, r0, r1 = ranks(id_line, 1)
    slot = lax.broadcasted_iota(jnp.int32, (TOK, ROWS), 1)
    row0, row1 = split_row(id0, r0), split_row(id1, r1)
    s0, s1 = shares(logits)
    for c in range(3):
        cols = slice(c * THIRD, (c + 1) * THIRD)
        pick0 = (slot == row0 + c * SLOT).astype(F32).astype(BF)
        pick1 = (slot == row1 + c * SLOT).astype(F32).astype(BF)
        first = jnp.dot(pick0, answers[...], preferred_element_type=F32)
        second = jnp.dot(pick1, answers[...], preferred_element_type=F32)
        out[:, cols] = (att[:, cols].astype(F32) + first * s0 + second * s1).astype(BF)


def combine_kernel(answers, att, logits, id_line, out):
    id0, id1, r0, r1 = ranks(id_line, 1)
    slot = lax.broadcasted_iota(jnp.int32, (TOK, NCTX * SLOTS), 1)
    pick0 = (slot == id0 * SLOTS + r0).astype(F32).astype(BF)
    pick1 = (slot == id1 * SLOTS + r1).astype(F32).astype(BF)
    s0, s1 = shares(logits)
    first = jnp.dot(pick0, answers[...], preferred_element_type=F32) * s0
    second = jnp.dot(pick1, answers[...], preferred_element_type=F32) * s1
    out[...] = (att[...].astype(F32) + first + second).astype(BF)


def place_rows(att, id_line):
    return pl.pallas_call(
        place_kernel,
        name="place_rows",
        out_shape=jax.ShapeDtypeStruct((NCTX * SLOTS, att.shape[1]), BF),
        in_specs=[VM] * 2,
        out_specs=VM,
        compiler_params=room(8),
    )(att, id_line)


def combine(kernel, answers, att, logits, id_line):
    return pl.pallas_call(
        kernel,
        name="combine",
        out_shape=jax.ShapeDtypeStruct(att.shape, BF),
        in_specs=[VM] * 4,
        out_specs=VM,
        compiler_params=room(10),
    )(answers, att, logits, id_line)


def swap(x, axis):
    return lax.all_to_all(x, axis, 0, 0, tiled=True)


def swap_y(x):
    return lax.all_to_all(x, "ep", 0, 0, axis_index_groups=Y_GROUPS, tiled=True)


def owners_only(args):
    att, _, gate_weight, up_weight, down_weight, _, _, _, _, _, id_line, logits = args
    outgoing = place_rows(att, id_line).reshape(NCTX, SLOTS, att.shape[1])
    arrived = swap(outgoing, "ctx")
    parts = swap(gate_up(arrived.reshape(NCTX * SLOTS, -1), gate_weight, up_weight), "ep")
    produced = down(swap(hidden(parts), "ep"), down_weight)
    back = swap(produced.reshape(NCTX, SLOTS, -1), "ctx")
    return combine(combine_kernel, back.reshape(NCTX * SLOTS, -1), att, logits, id_line)


def both_cores(args):
    att, placed, wg, wu, wd, sg, su, sd, own, side, id_line, logits = args
    arrived = swap(placed.reshape(NCTX, SPAN, THIRD), "ctx").reshape(ROWS, THIRD)
    leave, stay, cross = split_gate_up(own, side, arrived, wg, wu, sg, su)
    came = lax.ppermute(leave, "ep", X_PAIRS)
    crossed = swap_y(cross.reshape(NY, 2 * HALF, -1)).reshape(cross.shape)
    onward, leave, keep = middle(side, stay, came, crossed)
    came = lax.ppermute(leave, "ep", X_PAIRS)
    pieces = split_hidden(swap_y(onward), keep, came)
    produced = split_down(own, swap(pieces, "ep"), wd, sd)
    back = swap(produced.reshape(NCTX, SPAN, THIRD), "ctx").reshape(ROWS, THIRD)
    return combine(split_combine_kernel, back, att, logits, id_line)


def on_device(queries, keys, values, gate_weight, up_weight, down_weight, expert_ids, route_logits):
    my = lax.axis_index("ctx").astype(jnp.int32).reshape(1)
    side = (lax.axis_index("ep") % 2).astype(jnp.int32).reshape(1)
    id_line, logits = expert_ids.T, route_logits.T
    keys2, values2 = [lax.ppermute(a, "ctx", CORE_PAIRS) for a in (keys, values)]
    kv, own, one_chip = prepare(my, keys, values, keys2, values2, id_line)
    weights = (gate_weight, up_weight, down_weight)
    held = lax.optimization_barrier((kv,) + weights)
    theirs = [lax.ppermute(w, "ctx", CORE_PAIRS) for w in held[1:]]
    ka, kb, kc, kd, q6 = gather_kv(kv, queries)
    att, placed = attend(my, q6, ka, kb, kc, kd, id_line)
    args = (att, placed, *weights, *theirs, own, side, id_line, logits)
    return lax.cond(one_chip[0] == 1, owners_only, both_cores, args)


def solution(mesh):
    in_specs = (
        P("ctx", "ep"),
        P("ctx", "ep"),
        P("ctx", "ep"),
        P("ctx", "ep", None),
        P("ctx", "ep", None),
        P("ctx", None, "ep"),
        P("ctx", None),
        P("ctx", None),
    )
    return jax.shard_map(
        on_device, mesh=mesh, in_specs=in_specs, out_specs=P("ctx", "ep"), check_vma=False
    )
```

```python
import functools

import jax
import jax.numpy as jnp
from jax import lax
from jax.experimental import pallas as pl
from jax.experimental.pallas import tpu as pltpu
from jax.sharding import PartitionSpec as P


BF = jnp.bfloat16
F32 = jnp.float32
H = 48
KVH = 8
HD = 128
TOK = 128
NCTX = 32
NEP = 8
SLOTS = 24
Z = 8
NEG = -1e30
LOG2E = 1.4426950408889634
BLOCKS = 4
CAP = 12
THIRD = 256
SLOT = 18
SPAN = 56
ROWS = NCTX * SPAN
COLD = NCTX * CAP
EXTRA = NCTX * (SLOT - CAP)
TILE = 64
NY = NEP // 2
HALF = (COLD + EXTRA) // 2
VM = pl.BlockSpec(memory_space=pltpu.VMEM)
ANY = pl.BlockSpec(memory_space=pl.ANY)
HBM = pl.BlockSpec(memory_space=pltpu.HBM)
SM = pl.BlockSpec(memory_space=pltpu.SMEM)


def hold(x):
    return pltpu.with_memory_space_constraint(x, pltpu.HBM)


def room(mib):
    return pltpu.CompilerParams(vmem_limit_bytes=mib * 1024 * 1024)


def place(xl, z, c):
    return xl * 2 * Z + z * 2 + c


def z_step(core, i):
    return i + 1 if core == 0 else -i


def z_shift(i):
    return [
        (place(xl, z, c), place(xl, (z + z_step(c, i)) % Z, c))
        for xl in range(2)
        for z in range(Z)
        for c in range(2)
    ]


X_PAIRS = [(i, i ^ 1) for i in range(NEP)]
Y_GROUPS = [[2 * y + x for y in range(NEP // 2)] for x in range(2)]
CORE_PAIRS = [(i, i ^ 1) for i in range(NCTX)]
XLO_PAIRS = [(i, i ^ (2 * Z)) for i in range(NCTX)]
ORDER = (3, 2, 1, 0)


def prepare_kernel(my, keys, values, keys2, values2, id_line, kv, own, alone, sem):
    loads = [
        pltpu.make_async_copy(keys, kv.at[:TOK, :HD], sem.at[0]),
        pltpu.make_async_copy(values, kv.at[:TOK, HD:], sem.at[1]),
    ]
    for load in loads:
        load.start()
    kv[TOK:, :HD] = keys2[...]
    kv[TOK:, HD:] = values2[...]
    expert = lax.broadcasted_iota(jnp.int32, (NCTX, TOK), 0)
    named = (expert == id_line[0:1, :]).astype(F32) + (expert == id_line[1:2, :]).astype(F32)
    hot = (jnp.sum(named, axis=1, keepdims=True) > CAP).astype(jnp.int32)
    place_of = lax.broadcasted_iota(jnp.int32, (NCTX, 1), 0)
    own[0] = jnp.sum(hot * (place_of == my[0]).astype(jnp.int32))
    chip = hot * (place_of >> 1)
    low = jnp.max(chip + (1 - hot) * -1)
    high = jnp.min(chip + (1 - hot) * NCTX)
    alone[0] = (low == high).astype(jnp.int32)
    for load in loads:
        load.wait()


def prepare(my, keys, values, keys2, values2, id_line):
    keys, values = hold(keys), hold(values)
    return pl.pallas_call(
        prepare_kernel,
        name="prepare",
        out_shape=(
            jax.ShapeDtypeStruct((2 * TOK, 2 * HD), BF),
            jax.ShapeDtypeStruct((1,), jnp.int32),
            jax.ShapeDtypeStruct((1,), jnp.int32),
        ),
        in_specs=[SM, HBM, HBM] + [VM] * 3,
        out_specs=(VM,) + (pl.BlockSpec(memory_space=pltpu.SMEM),) * 2,
        scratch_shapes=[pltpu.SemaphoreType.DMA((2,))],
        compiler_params=room(8),
    )(my, keys, values, keys2, values2, id_line)


def join_kernel(*refs):
    out = refs[-1]
    for b, ref in enumerate(refs[:-1]):
        out[b * 2 * TOK : (b + 1) * 2 * TOK] = ref[...]


def join(blocks):
    return pl.pallas_call(
        join_kernel,
        name="join",
        out_shape=jax.ShapeDtypeStruct((len(blocks) * 2 * TOK, 2 * HD), BF),
        in_specs=[VM] * len(blocks),
        out_specs=VM,
        compiler_params=room(6),
    )(*blocks)


def join_near_kernel(q, *refs):
    out, q6, sem = refs[-3:]
    loads = [
        pltpu.make_async_copy(
            q.at[:, h * HD : (h + 1) * HD], q6.at[h * TOK : (h + 1) * TOK], sem.at[h]
        )
        for h in range(6)
    ]
    for load in loads:
        load.start()
    join_kernel(*refs[:-2])
    for load in loads:
        load.wait()


def join_near(q, blocks):
    q = hold(q)
    return pl.pallas_call(
        join_near_kernel,
        name="join_near",
        out_shape=(
            jax.ShapeDtypeStruct((len(blocks) * 2 * TOK, 2 * HD), BF),
            jax.ShapeDtypeStruct((6 * TOK, HD), BF),
        ),
        in_specs=[HBM] + [VM] * len(blocks),
        out_specs=(VM, VM),
        scratch_shapes=[pltpu.SemaphoreType.DMA((6,))],
        compiler_params=room(6),
    )(q, *blocks)


def gather_kv(kv, q):
    near = [lax.ppermute(kv, "ctx", z_shift(i)) for i in ORDER]
    far = [lax.ppermute(block, "ctx", XLO_PAIRS) for block in near]
    ka, q6 = join_near(q, near)
    kb = join(far)
    kc, kd = [lax.ppermute(part, "ctx", CORE_PAIRS) for part in (ka, kb)]
    return ka, kb, kc, kd, q6


def column(line):
    return jnp.transpose(jnp.broadcast_to(line.astype(F32), (TOK, TOK)))[:, 0:1]


def ranks(id_line, axis):
    a = lax.broadcasted_iota(jnp.int32, (TOK, TOK), axis)
    b = lax.broadcasted_iota(jnp.int32, (TOK, TOK), 1 - axis)
    before = a < b
    line0, line1 = id_line[0:1, :].astype(F32), id_line[1:2, :].astype(F32)
    col0, col1 = column(line0), column(line1)
    if axis == 0:
        own0, own1, oth0, oth1 = line0, line1, col0, col1
    else:
        own0, own1, oth0, oth1 = col0, col1, line0, line1

    def count(mask):
        return jnp.sum(mask.astype(F32), axis=axis, keepdims=True).astype(jnp.int32)

    rank0 = count((oth0 == own0) & before)
    rank1 = count(oth0 == own1) + count((oth1 == own1) & before)
    return own0.astype(jnp.int32), own1.astype(jnp.int32), rank0, rank1


def split_row(expert, rank):
    over = (rank >= SLOT).astype(jnp.int32)
    return (expert ^ over) * SPAN + rank - (SLOT - CAP) * over


def slot_map(c, extra, transposed):
    count = SLOT - CAP if extra else CAP
    rows, cols = 8 * count, 8 * SPAN
    shape = (cols, rows) if transposed else (rows, cols)
    i = lax.broadcasted_iota(jnp.int32, shape, 1 if transposed else 0)
    j = lax.broadcasted_iota(jnp.int32, shape, 0 if transposed else 1)
    source = (i * (43 if count == CAP else 86)) >> 9
    slot = i - source * count + (CAP if extra else 0)
    return (j == source * SPAN + c * SLOT + slot).astype(F32).astype(BF)


def place_kernel(att, id_line, placed):
    id0, id1, r0, r1 = ranks(id_line, 0)
    slot = lax.broadcasted_iota(jnp.int32, (NCTX * SLOTS, TOK), 0)
    pick = (slot == id0 * SLOTS + r0) | (slot == id1 * SLOTS + r1)
    pick = pick.astype(F32).astype(BF)
    placed[...] = jnp.dot(pick, att[...], preferred_element_type=F32).astype(BF)


def attend_kernel(
    my_ref, q6, ka, kb, kc, kd, id_line, att, placed, s, m, total, acc, meta
):
    my = my_ref[0]
    xl, z, core = my // (2 * Z), (my // 2) % Z, my % 2
    at = 0
    for cc in (core, 1 - core):
        for xx in (xl, 1 - xl):
            for i in ORDER:
                step = jnp.where(cc == 0, i + 1, -i)
                for which in (cc, 1 - cc):
                    meta[at] = (place(xx, (z + Z - step) % Z, which) - my) * TOK
                    at += 1
    m[...] = jnp.full_like(m, NEG)
    gap = (lax.broadcasted_iota(jnp.int32, (6 * TOK, TOK), 0) & (TOK - 1)) - lax.broadcasted_iota(
        jnp.int32, (6 * TOK, TOK), 1
    )
    scale = HD ** (-0.5) * LOG2E
    quarter = NCTX // 4 * TOK
    wide = BLOCKS * TOK
    for side, kv in enumerate((ka, kb, kc, kd)):

        def scores(i, carry):
            rows = pl.ds(pl.multiple_of(i * wide, wide), wide)
            cols = pl.ds(pl.multiple_of(side * quarter + i * wide, wide), wide)
            value = lax.dot_general(
                q6[...], kv[rows, 0:HD], (((1,), (1,)), ((), ())), preferred_element_type=F32
            )
            base = side * (NCTX // 4) + i * BLOCKS
            pieces = [
                jnp.where(gap >= meta[base + b], value[:, b * TOK : (b + 1) * TOK], NEG)
                for b in range(BLOCKS)
            ]
            s[:, cols] = jnp.concatenate(pieces, axis=1)
            m[...] = jnp.maximum(m[...], functools.reduce(jnp.maximum, pieces))
            return carry

        lax.fori_loop(0, NCTX // 4 // BLOCKS, scores, 0)
    top = jnp.broadcast_to(jnp.max(m[...], axis=1, keepdims=True), (6 * TOK, TOK))
    m[...] = top
    total[...] = jnp.zeros_like(total)
    acc[...] = jnp.zeros_like(acc)
    for side, kv in enumerate((ka, kb, kc, kd)):

        def mix(i, carry):
            rows = pl.ds(pl.multiple_of(i * wide, wide), wide)
            cols = pl.ds(pl.multiple_of(side * quarter + i * wide, wide), wide)
            part = s[:, cols]
            top = m[...]
            pieces = [
                jnp.exp2((part[:, b * TOK : (b + 1) * TOK] - top) * scale) for b in range(BLOCKS)
            ]
            total[...] += functools.reduce(jnp.add, pieces)
            p = jnp.concatenate([piece.astype(BF) for piece in pieces], axis=1)
            acc[...] += jnp.dot(p, kv[rows, HD:], preferred_element_type=F32)
            return carry

        lax.fori_loop(0, NCTX // 4 // BLOCKS, mix, 0)
    out = (acc[...] / jnp.sum(total[...], axis=1, keepdims=True)).astype(BF)
    for h in range(6):
        att[:, h * HD : (h + 1) * HD] = out[h * TOK : (h + 1) * TOK]
    id0, id1, r0, r1 = ranks(id_line, 0)
    slot = lax.broadcasted_iota(jnp.int32, (ROWS, TOK), 0)
    row0, row1 = split_row(id0, r0), split_row(id1, r1)
    filled = jnp.zeros((ROWS, THIRD), F32)
    for c in range(3):
        pick = (slot == row0 + c * SLOT) | (slot == row1 + c * SLOT)
        pick = pick.astype(F32).astype(BF)
        filled += jnp.dot(pick, att[:, c * THIRD : (c + 1) * THIRD], preferred_element_type=F32)
    placed[...] = filled.astype(BF)


def attend(my, q, ka, kb, kc, kd, id_line):
    return pl.pallas_call(
        attend_kernel,
        name="attend",
        out_shape=(
            jax.ShapeDtypeStruct((TOK, 6 * HD), BF),
            jax.ShapeDtypeStruct((ROWS, THIRD), BF),
        ),
        in_specs=[pl.BlockSpec(memory_space=pltpu.SMEM)] + [VM] * 6,
        out_specs=(VM, VM),
        scratch_shapes=[
            pltpu.VMEM((6 * TOK, NCTX * TOK), F32),
            pltpu.VMEM((6 * TOK, TOK), F32),
            pltpu.VMEM((6 * TOK, TOK), F32),
            pltpu.VMEM((6 * TOK, HD), F32),
            pltpu.SMEM((NCTX,), jnp.int32),
        ],
        compiler_params=room(28),
    )(my, q, ka, kb, kc, kd, id_line)


def gate_up_kernel(x, wg, wu, out):
    width = wg.shape[2]
    out[0, :, :width] = jnp.dot(x[...], wg[0], preferred_element_type=F32).astype(BF)
    out[0, :, width:] = jnp.dot(x[...], wu[0], preferred_element_type=F32).astype(BF)


def gate_up(x, wg, wu):
    rows, depth = x.shape
    width = wg.shape[2] // NEP
    weight = pl.BlockSpec((1, depth, width), lambda j: (0, 0, j))
    return pl.pallas_call(
        gate_up_kernel,
        name="gate_up",
        grid=(NEP,),
        out_shape=jax.ShapeDtypeStruct((NEP, rows, 2 * width), BF),
        in_specs=[pl.BlockSpec((rows, depth), lambda j: (0, 0)), weight, weight],
        out_specs=pl.BlockSpec((1, rows, 2 * width), lambda j: (j, 0, 0)),
        compiler_params=room(24),
    )(x, wg, wu)


def hidden_kernel(parts, out):
    width = out.shape[2]
    total = parts[0].astype(F32)
    for j in range(1, NEP):
        total += parts[j].astype(F32)
    gate, up = total[:, :width], total[:, width:]
    value = (gate / (1.0 + jnp.exp(-gate)) * up).astype(BF)
    for j in range(NEP):
        out[j] = value


def hidden(parts):
    _, rows, width = parts.shape
    tile = TILE if rows % 192 else 192
    return pl.pallas_call(
        hidden_kernel,
        name="hidden",
        grid=(rows // tile,),
        out_shape=jax.ShapeDtypeStruct((NEP, rows, width // 2), BF),
        in_specs=[pl.BlockSpec((NEP, tile, width), lambda i: (0, i, 0))],
        out_specs=pl.BlockSpec((NEP, tile, width // 2), lambda i: (0, i, 0)),
        compiler_params=room(12),
    )(parts)


def down_kernel(h, w, out, acc):
    j = pl.program_id(0)
    part = jnp.dot(h[0], w[0], preferred_element_type=F32)

    @pl.when(j == 0)
    def _():
        acc[...] = part

    @pl.when(j > 0)
    def _():
        acc[...] += part

    @pl.when(j == NEP - 1)
    def _():
        out[...] = acc[...].astype(BF)


def down(h, w):
    _, rows, width = h.shape
    cols = w.shape[2]
    return pl.pallas_call(
        down_kernel,
        name="down",
        grid=(NEP,),
        out_shape=jax.ShapeDtypeStruct((rows, cols), BF),
        in_specs=[
            pl.BlockSpec((1, rows, width), lambda j: (j, 0, 0)),
            pl.BlockSpec((1, width, cols), lambda j: (0, j, 0)),
        ],
        out_specs=pl.BlockSpec((rows, cols), lambda j: (0, 0)),
        scratch_shapes=[pltpu.VMEM((rows, cols), F32)],
        compiler_params=room(16),
    )(h, w)


def split_gate_up_kernel(
    own, side, arr, wg, wu, sg, su, leave_out, stay_out, cross_out, x, bg, bu, cg, cu,
    leave, stay, cross, sem, done
):
    loads = [
        pltpu.make_async_copy(wg.at[0], bg, sem.at[0]),
        pltpu.make_async_copy(wu.at[0], bu, sem.at[1]),
        pltpu.make_async_copy(sg.at[0], cg, sem.at[2]),
        pltpu.make_async_copy(su.at[0], cu, sem.at[3]),
    ]
    for load in loads[:2]:
        load.start()
    width = wg.shape[2] // NEP
    n, m = 8 * CAP, 8 * (SLOT - CAP)
    for c in range(3):
        cols = slice(c * THIRD, (c + 1) * THIRD)
        cold, extra = slot_map(c, False, False), slot_map(c, True, False)
        for g in range(NCTX // 8):
            group = arr[g * 8 * SPAN : (g + 1) * 8 * SPAN]
            x[g * n : (g + 1) * n, cols] = jnp.dot(
                cold, group, preferred_element_type=F32
            ).astype(BF)
            x[COLD + g * m : COLD + (g + 1) * m, cols] = jnp.dot(
                extra, group, preferred_element_type=F32
            ).astype(BF)

    mine = side[0]

    def cold_piece(at, w):
        for kept, part in ((0, leave), (1, stay)):
            to = mine if kept else 1 - mine
            for y in range(NY):
                cols = pl.ds(pl.multiple_of((2 * y + to) * width, width), width)
                value = jnp.dot(x[:COLD], w[:, cols], preferred_element_type=F32).astype(BF)
                part[y, :, at : at + width] = value[:HALF]
                cross[y, to, : COLD - HALF, at : at + width] = value[HALF:]

    def extra_piece(y, first, second):
        for j in (2 * y, 2 * y + 1):
            for at, w in ((0, first), (width, second)):
                cross[y, j % 2, COLD - HALF :, at : at + width] = jnp.dot(
                    x[COLD:], w[:, j * width : (j + 1) * width], preferred_element_type=F32
                ).astype(BF)

    loads[0].wait()
    loads[2].start()
    cold_piece(0, bg)
    loads[1].wait()
    loads[3].start()
    cold_piece(width, bu)
    stores = [
        pltpu.make_async_copy(leave, leave_out, done.at[0]),
        pltpu.make_async_copy(stay, stay_out, done.at[1]),
    ]
    for store in stores:
        store.start()
    loads[2].wait()
    loads[3].wait()
    for y in range(NY):

        @pl.when(own[0] == 1)
        def _():
            extra_piece(y, bg, bu)

        @pl.when(own[0] == 0)
        def _():
            extra_piece(y, cg, cu)

        store = pltpu.make_async_copy(cross.at[y], cross_out.at[y], done.at[2 + y])
        store.start()
        stores.append(store)
    for store in stores:
        store.wait()


def split_gate_up(own, side, arr, wg, wu, sg, su):
    _, depth, full = wg.shape
    rows = COLD + EXTRA
    return pl.pallas_call(
        split_gate_up_kernel,
        name="split_gate_up",
        out_shape=(
            pltpu.HBM((NY, HALF, 2 * full // NEP), BF),
            pltpu.HBM((NY, HALF, 2 * full // NEP), BF),
            pltpu.HBM((NY, 2, HALF, 2 * full // NEP), BF),
        ),
        in_specs=[SM, SM, VM, ANY, ANY, ANY, ANY],
        out_specs=(HBM, HBM, HBM),
        scratch_shapes=[
            pltpu.VMEM((rows, depth), BF),
            pltpu.VMEM((depth, full), BF),
            pltpu.VMEM((depth, full), BF),
            pltpu.VMEM((depth, full), BF),
            pltpu.VMEM((depth, full), BF),
            pltpu.VMEM((NY, HALF, 2 * full // NEP), BF),
            pltpu.VMEM((NY, HALF, 2 * full // NEP), BF),
            pltpu.VMEM((NY, 2, HALF, 2 * full // NEP), BF),
            pltpu.SemaphoreType.DMA((4,)),
            pltpu.SemaphoreType.DMA((2 + NY,)),
        ],
        compiler_params=room(26),
    )(own, side, arr, wg, wu, sg, su)


def middle_kernel(side, stay, came, cross, onward, leave, keep):
    for y in range(NY):
        onward[y] = (stay[y].astype(F32) + came[y].astype(F32)).astype(BF)
    for to, part in ((1 - side[0], leave), (side[0], keep)):
        total = cross[0, to].astype(F32)
        for y in range(1, NY):
            total += cross[y, to].astype(F32)
        part[...] = total.astype(BF)


def middle(side, stay, came, cross):
    _, rows, width = stay.shape
    tile = rows
    quad = pl.BlockSpec((NY, tile, width), lambda i: (0, i, 0))
    single = pl.BlockSpec((tile, width), lambda i: (i, 0))
    return pl.pallas_call(
        middle_kernel,
        name="middle",
        grid=(1,),
        out_shape=(
            pltpu.HBM(stay.shape, BF),
            pltpu.HBM((rows, width), BF),
            pltpu.HBM((rows, width), BF),
        ),
        in_specs=[SM, quad, quad, pl.BlockSpec((NY, 2, tile, width), lambda i: (0, 0, i, 0))],
        out_specs=(quad, single, single),
        compiler_params=room(24),
    )(side, hold(stay), hold(came), cross)


def split_hidden_kernel(onward, keep, came, out):
    rows, width = keep.shape
    tile = rows // 3
    half = width // 2

    def finish(total, at):
        gate, up = total[:, :half], total[:, half:]
        value = (gate / (1.0 + jnp.exp(-gate)) * up).astype(BF)
        for j in range(NEP):
            out[j, at : at + tile] = value

    for lo in range(0, rows, tile):
        total = onward[0, lo : lo + tile].astype(F32)
        for y in range(1, NY):
            total += onward[y, lo : lo + tile].astype(F32)
        finish(total, lo)
        total = keep[lo : lo + tile].astype(F32) + came[lo : lo + tile].astype(F32)
        finish(total, rows + lo)


def split_hidden(onward, keep, came):
    rows, width = keep.shape
    return pl.pallas_call(
        split_hidden_kernel,
        name="split_hidden",
        out_shape=jax.ShapeDtypeStruct((NEP, 2 * rows, width // 2), BF),
        in_specs=[VM] * 3,
        out_specs=VM,
        compiler_params=room(10),
    )(onward, keep, came)


def split_down_kernel(own, h, w, v, out, wide, y, theirs, sem):
    load = pltpu.make_async_copy(v, theirs, sem)
    load.start()
    width = h.shape[2]
    for j in range(NEP):
        wide[:, j * width : (j + 1) * width] = h[j]

    def product(lo, hi, weights):
        for c in range(3):
            cols = slice(c * THIRD, (c + 1) * THIRD)
            y[lo:hi, cols] = jnp.dot(
                wide[lo:hi], weights[0, :, cols], preferred_element_type=F32
            ).astype(BF)

    product(0, COLD, w)
    load.wait()

    @pl.when(own[0] == 1)
    def _():
        product(COLD, COLD + EXTRA, w)

    @pl.when(own[0] == 0)
    def _():
        product(COLD, COLD + EXTRA, theirs)

    n, m = 8 * CAP, 8 * (SLOT - CAP)
    maps = [(slot_map(c, False, True), slot_map(c, True, True)) for c in range(3)]
    for g in range(NCTX // 8):
        total = jnp.zeros((8 * SPAN, THIRD), F32)
        for c in range(3):
            cols = slice(c * THIRD, (c + 1) * THIRD)
            cold, extra = maps[c]
            total += jnp.dot(cold, y[g * n : (g + 1) * n, cols], preferred_element_type=F32)
            total += jnp.dot(
                extra, y[COLD + g * m : COLD + (g + 1) * m, cols], preferred_element_type=F32
            )
        out[g * 8 * SPAN : (g + 1) * 8 * SPAN] = total.astype(BF)


def split_down(own, h, w, v):
    _, rows, width = h.shape
    _, depth, cols = w.shape
    return pl.pallas_call(
        split_down_kernel,
        name="split_down",
        out_shape=jax.ShapeDtypeStruct((ROWS, THIRD), BF),
        in_specs=[pl.BlockSpec(memory_space=pltpu.SMEM), VM, VM, ANY],
        out_specs=VM,
        scratch_shapes=[
            pltpu.VMEM((rows, depth), BF),
            pltpu.VMEM((rows, cols), BF),
            pltpu.VMEM(v.shape, BF),
            pltpu.SemaphoreType.DMA,
        ],
        compiler_params=room(20),
    )(own, h, w, v)


def shares(logits):
    l0, l1 = column(logits[0:1, :]), column(logits[1:2, :])
    top = jnp.maximum(l0, l1)
    e0, e1 = jnp.exp(l0 - top), jnp.exp(l1 - top)
    both = e0 + e1
    return e0 / both, e1 / both


def split_combine_kernel(answers, att, logits, id_line, out):
    id0, id1, r0, r1 = ranks(id_line, 1)
    slot = lax.broadcasted_iota(jnp.int32, (TOK, ROWS), 1)
    row0, row1 = split_row(id0, r0), split_row(id1, r1)
    s0, s1 = shares(logits)
    for c in range(3):
        cols = slice(c * THIRD, (c + 1) * THIRD)
        pick0 = (slot == row0 + c * SLOT).astype(F32).astype(BF)
        pick1 = (slot == row1 + c * SLOT).astype(F32).astype(BF)
        first = jnp.dot(pick0, answers[...], preferred_element_type=F32)
        second = jnp.dot(pick1, answers[...], preferred_element_type=F32)
        out[:, cols] = (att[:, cols].astype(F32) + first * s0 + second * s1).astype(BF)


def combine_kernel(answers, att, logits, id_line, out):
    id0, id1, r0, r1 = ranks(id_line, 1)
    slot = lax.broadcasted_iota(jnp.int32, (TOK, NCTX * SLOTS), 1)
    pick0 = (slot == id0 * SLOTS + r0).astype(F32).astype(BF)
    pick1 = (slot == id1 * SLOTS + r1).astype(F32).astype(BF)
    s0, s1 = shares(logits)
    first = jnp.dot(pick0, answers[...], preferred_element_type=F32) * s0
    second = jnp.dot(pick1, answers[...], preferred_element_type=F32) * s1
    out[...] = (att[...].astype(F32) + first + second).astype(BF)


def place_rows(att, id_line):
    return pl.pallas_call(
        place_kernel,
        name="place_rows",
        out_shape=jax.ShapeDtypeStruct((NCTX * SLOTS, att.shape[1]), BF),
        in_specs=[VM] * 2,
        out_specs=VM,
        compiler_params=room(8),
    )(att, id_line)


def combine(kernel, answers, att, logits, id_line):
    return pl.pallas_call(
        kernel,
        name="combine",
        out_shape=jax.ShapeDtypeStruct(att.shape, BF),
        in_specs=[VM] * 4,
        out_specs=VM,
        compiler_params=room(10),
    )(answers, att, logits, id_line)


def swap(x, axis):
    return lax.all_to_all(x, axis, 0, 0, tiled=True)


def swap_y(x):
    return lax.all_to_all(x, "ep", 0, 0, axis_index_groups=Y_GROUPS, tiled=True)


def owners_only(args):
    att, _, gate_weight, up_weight, down_weight, _, _, _, _, _, id_line, logits = args
    outgoing = place_rows(att, id_line).reshape(NCTX, SLOTS, att.shape[1])
    arrived = swap(outgoing, "ctx")
    parts = swap(gate_up(arrived.reshape(NCTX * SLOTS, -1), gate_weight, up_weight), "ep")
    produced = down(swap(hidden(parts), "ep"), down_weight)
    back = swap(produced.reshape(NCTX, SLOTS, -1), "ctx")
    return combine(combine_kernel, back.reshape(NCTX * SLOTS, -1), att, logits, id_line)


def both_cores(args):
    att, placed, wg, wu, wd, sg, su, sd, own, side, id_line, logits = args
    arrived = swap(placed.reshape(NCTX, SPAN, THIRD), "ctx").reshape(ROWS, THIRD)
    leave, stay, cross = split_gate_up(own, side, arrived, wg, wu, sg, su)
    came = lax.ppermute(leave, "ep", X_PAIRS)
    crossed = swap_y(cross.reshape(NY, 2 * HALF, -1)).reshape(cross.shape)
    onward, leave, keep = middle(side, stay, came, crossed)
    came = lax.ppermute(leave, "ep", X_PAIRS)
    pieces = split_hidden(swap_y(onward), keep, came)
    produced = split_down(own, swap(pieces, "ep"), wd, sd)
    back = swap(produced.reshape(NCTX, SPAN, THIRD), "ctx").reshape(ROWS, THIRD)
    return combine(split_combine_kernel, back, att, logits, id_line)


def on_device(queries, keys, values, gate_weight, up_weight, down_weight, expert_ids, route_logits):
    my = lax.axis_index("ctx").astype(jnp.int32).reshape(1)
    side = (lax.axis_index("ep") % 2).astype(jnp.int32).reshape(1)
    id_line, logits = expert_ids.T, route_logits.T
    keys2, values2 = [lax.ppermute(a, "ctx", CORE_PAIRS) for a in (keys, values)]
    kv, own, one_chip = prepare(my, keys, values, keys2, values2, id_line)
    weights = (gate_weight, up_weight, down_weight)
    held = lax.optimization_barrier((kv,) + weights)
    theirs = [lax.ppermute(w, "ctx", CORE_PAIRS) for w in held[1:]]
    ka, kb, kc, kd, q6 = gather_kv(kv, queries)
    att, placed = attend(my, q6, ka, kb, kc, kd, id_line)
    args = (att, placed, *weights, *theirs, own, side, id_line, logits)
    return lax.cond(one_chip[0] == 1, owners_only, both_cores, args)


def solution(mesh):
    in_specs = (
        P("ctx", "ep"),
        P("ctx", "ep"),
        P("ctx", "ep"),
        P("ctx", "ep", None),
        P("ctx", "ep", None),
        P("ctx", None, "ep"),
        P("ctx", None),
        P("ctx", None),
    )
    return jax.shard_map(
        on_device, mesh=mesh, in_specs=in_specs, out_specs=P("ctx", "ep"), check_vma=False
    )
```
